256 devices in a mesh: dp: 8 (over z), ctx: 32 (over x, y, core).
Axes of the slice: x: 4, y: 4, z: 8, core: 2. Of those that a mesh axis runs over, the one named last changes fastest.
Arguments:
- head_inputs: bfloat16 [8, 4096, 2048], P('dp', 'ctx'), may hold values from -11 to 11
- entry_operator: bfloat16 [8, 4096, 128], P('dp', 'ctx'), may hold values from -3 to 3
- memory_readout: bfloat16 [8, 4096, 128], P('dp', 'ctx'), may hold values from -0.1796875 to 0.1796875
- unshifted_strides: float32 [8, 64, 4096], P('dp', None, 'ctx'), may hold values from -1.5 to 5.5, as said below
- log_decay_rates: float32 [64], P('dp'), may hold values from -11 to -2
- stride_shift: float32 [64], P('dp'), may hold values from -0.5 to 0.5
- bypass_coefficients: float32 [64], P('dp'), may hold values from 0.5 to 1.5
- result_cotangent: bfloat16 [8, 4096, 2048], P('dp', 'ctx'), may hold values from -26 to 26
Outputs:
- output: bfloat16 [8, 4096, 2048], P('dp', 'ctx')
- channels_grad: bfloat16 [8, 4096, 2048], P('dp', 'ctx')
- input_map_grad: float32 [8, 4096, 128], P('dp', 'ctx')
- output_map_grad: float32 [8, 4096, 128], P('dp', 'ctx')
- timestep_raw_gradient: float32 [8, 64, 4096], P('dp', None, 'ctx')
- a_log_grad: float32 [64], P('dp')
- bias_grad: float32 [64], P('dp')
- skip_grad: float32 [64], P('dp')
The draws below stay inside these ranges and needn't reach their ends.
Inputs may be any that keep to these rules, and one draw needn't show every extreme that they name: `unshifted_strides`: step sizes are moderate at most positions, with a few large ones in each sequence.
All inputs are finite; a program needn't handle non-finite values.
Results may differ from the reference program's by a relative error of at most 0.001.
Values sent between devices are 32-bit elements; how exact they have to be, the bound alone decides.
A program may use at most 128 MiB of HBM per device.

```python
import jax
import jax.numpy as jnp
from jax import lax

HEADS = 64
HEAD_DIM = 32
MEMORY_WIDTH = 128
TOK_DEV = 128
WINDOW_LENGTH = 4096
BATCH_COUNT = 8


def block_levels(key):
    level_key = jax.random.fold_in(key, 71)
    blocks = WINDOW_LENGTH // TOK_DEV
    exponent = jax.random.uniform(level_key, (BATCH_COUNT, blocks), jnp.float32, -2.5, 1.0)
    return jnp.repeat(jnp.exp(exponent), TOK_DEV, axis=1)


def draw_head_inputs(key, part):
    first = jax.random.fold_in(key, 53)
    shape = (BATCH_COUNT, WINDOW_LENGTH, HEADS * HEAD_DIM)
    noise = jnp.clip(jax.random.normal(first, shape, jnp.float32), -4.0, 4.0)
    levels = block_levels(key)
    return (noise * levels[:, :, None]).astype(jnp.bfloat16)


def draw_entry_operator(key, part):
    first = jax.random.fold_in(key, 59)
    shape = (BATCH_COUNT, WINDOW_LENGTH, MEMORY_WIDTH)
    noise = jnp.clip(jax.random.normal(first, shape, jnp.float32), -4.0, 4.0)
    levels = block_levels(key)
    value = noise * MEMORY_WIDTH ** (-0.5) * levels[:, :, None]
    return value.astype(jnp.bfloat16)


def draw_log_decay_rates(key, part):
    first, second = jax.random.split(jax.random.fold_in(key, 11), 2)
    spread = jax.random.uniform(first, (HEADS,), jnp.float32)
    ranks = jax.random.permutation(second, HEADS)
    quick_count = HEADS // 4
    middle_count = HEADS // 4
    quick = ranks < quick_count
    middle = jnp.logical_and(ranks >= quick_count, ranks < quick_count + middle_count)
    slow_rate = jnp.log(0.2 / WINDOW_LENGTH) + spread * jnp.log(10.0)
    quick_rate = jnp.log(0.035) + spread * jnp.log(2.0)
    middle_rate = jnp.log(0.0105) + spread * jnp.log(1.45)
    value = jnp.where(quick, quick_rate, jnp.where(middle, middle_rate, slow_rate))
    return value.astype(jnp.float32)


def draw_unshifted_strides(key, part):
    first, second = jax.random.split(jax.random.fold_in(key, 23), 2)
    starting_index = jnp.clip(0.5 * jax.random.normal(first, (BATCH_COUNT, HEADS, WINDOW_LENGTH), jnp.float32), -1.0, 1.0) - 0.5
    worker_places = jax.random.randint(second, (BATCH_COUNT, 4), 0, WINDOW_LENGTH)
    index_table = jnp.arange(WINDOW_LENGTH, dtype=jnp.int32)
    contiguous_spans = jnp.any(index_table[None, None, :] == worker_places[:, :, None], axis=1).astype(jnp.float32)
    return (starting_index + 4.0 * contiguous_spans[:, None, :]).astype(jnp.float32)


def draw_result_cotangent(key, part):
    first = jax.random.fold_in(key, 37)
    noise = jnp.clip(jax.random.normal(first, (BATCH_COUNT, WINDOW_LENGTH, HEADS * HEAD_DIM), jnp.float32), -4.0, 4.0)
    along = jnp.arange(WINDOW_LENGTH, dtype=jnp.float32) / (WINDOW_LENGTH - 1)
    spanning_parts = jnp.arange(BATCH_COUNT, dtype=jnp.float32) / max(BATCH_COUNT - 1, 1)
    ramp = 1.0 + 2.0 * along
    value = noise * ramp[None, :, None] * (1.0 + spanning_parts)[:, None, None]
    return value.astype(jnp.bfloat16)


def steps_of(key, shape, pieces, smallest, top_value):
    loudness = 1.0
    for position, parts in pieces:
        draws = jax.random.uniform(jax.random.fold_in(jax.random.fold_in(key, 6), position), (parts,), jnp.float32, smallest / len(pieces), top_value / len(pieces))
        loudness = loudness * jnp.repeat(jnp.exp(draws), shape[position] // parts).reshape((-1,) + (1,) * (len(shape) - 1 - position))
    return loudness


def scatter_about(rng, dims, scale, bound, pieces=(), kind=jnp.bfloat16):
    values = jax.random.normal(rng, dims, jnp.float32) * scale
    if len(pieces) > 0:
        values = steps_of(rng, dims, pieces, -0.22, 0.18) * values
    return jnp.clip(values, min=-bound, max=bound).astype(kind)


def setup_inputs(seed: int = 0) -> dict:
    key_list = jax.random.split(jax.random.key(seed), 9)
    head_inputs = draw_head_inputs(jax.random.fold_in(key_list[8], 71), 0)
    entry_operator = draw_entry_operator(jax.random.fold_in(key_list[8], 71), 0)
    memory_readout = scatter_about(key_list[2], (BATCH_COUNT, WINDOW_LENGTH, MEMORY_WIDTH), 0.03, 0.1796875, ((0, 8), (1, 32)))
    unshifted_strides = draw_unshifted_strides(jax.random.fold_in(key_list[8], 71), 0)
    log_decay_rates = draw_log_decay_rates(jax.random.fold_in(key_list[8], 71), 0)
    stride_shift = jnp.clip(jax.random.uniform(key_list[5], (HEADS,), jnp.float32, -0.5, 0.5) * steps_of(key_list[5], (HEADS,), ((0, 8),), -0.4, 0.0), -0.5, 0.5)
    bypass_coefficients = jnp.clip(0.5 + 1.0 * jax.random.uniform(key_list[6], (HEADS,), jnp.float32) ** steps_of(key_list[6], (HEADS,), ((0, 8),), -0.2, 0.2), 0.5, 1.5)
    result_cotangent = draw_result_cotangent(jax.random.fold_in(key_list[8], 71), 0)
    return dict(head_inputs=head_inputs, entry_operator=entry_operator, memory_readout=memory_readout, unshifted_strides=unshifted_strides, log_decay_rates=log_decay_rates, stride_shift=stride_shift, bypass_coefficients=bypass_coefficients, result_cotangent=result_cotangent)


maximal_accuracy = lax.Precision.HIGHEST

def local_part(xg, write_operator, gram, dtr, rate_log, bias, skip):
    count = xg.shape[0]
    heads = dtr.shape[0]
    xg3 = xg.reshape(count, heads, -1)
    step = jax.nn.softplus(dtr + bias[:, None])
    logdecay = -jnp.exp(rate_log)[:, None] * step
    cum = jnp.cumsum(logdecay, axis=1)
    rows = lax.broadcasted_iota(jnp.int32, (count, count), 0)
    cols = lax.broadcasted_iota(jnp.int32, (count, count), 1)
    diff = cum[:, :, None] - cum[:, None, :]
    seg = jnp.exp(jnp.where((rows >= cols)[None], diff, -jnp.inf))
    weights = gram[None] * seg * step[:, None, :]
    inner = jnp.einsum('hts,shp->thp', weights, xg3, precision=maximal_accuracy)
    y_part = inner + skip[None, :, None] * xg3
    tail = jnp.exp(cum[:, -1:] - cum) * step
    scaled = xg3 * tail.T[:, :, None]
    state = jnp.einsum('shp,sn->hpn', scaled, write_operator, precision=maximal_accuracy)
    return (y_part, state, jnp.exp(cum))

def token_series(xs, bm, cm, dtr, log_decay_rates, stride_shift, bypass_coefficients):
    length = xs.shape[0]
    blocks = length // TOK_DEV
    heads = dtr.shape[0]
    xb = xs.reshape(blocks, TOK_DEV, heads * HEAD_DIM)
    bb = bm.reshape(blocks, TOK_DEV, -1)
    cb = cm.reshape(blocks, TOK_DEV, -1)
    db = dtr.reshape(heads, blocks, TOK_DEV).transpose(1, 0, 2)

    def block_step(carry, items):
        xblk, bblk, cblk, dblk = items
        gram = jnp.dot(cblk, bblk.T, precision=maximal_accuracy)
        y_part, state, growth_factor = local_part(xblk, bblk, gram, dblk, log_decay_rates, stride_shift, bypass_coefficients)
        readout = jnp.einsum('tn,hpn->thp', cblk, carry, precision=maximal_accuracy)
        yblk = y_part + growth_factor.T[:, :, None] * readout
        carry_next = growth_factor[:, -1][:, None, None] * carry + state
        return (carry_next, yblk)
    start = jnp.zeros((heads, HEAD_DIM, bm.shape[1]), jnp.float32)
    _, ys = lax.scan(block_step, start, (xb, bb, cb, db))
    return ys.reshape(length, heads * HEAD_DIM)

def forward(xf, brain_float_kind, cf, dtr, log_decay_rates, stride_shift, bypass_coefficients):

    def single(items):
        return token_series(items[0], items[1], items[2], items[3], log_decay_rates, stride_shift, bypass_coefficients)
    return lax.map(single, (xf, brain_float_kind, cf, dtr))

def reference(head_inputs, entry_operator, memory_readout, unshifted_strides, log_decay_rates, stride_shift, bypass_coefficients, result_cotangent):
    xf = head_inputs.astype(jnp.float32)
    brain_float_kind = entry_operator.astype(jnp.float32)
    cf = memory_readout.astype(jnp.float32)
    core, backward = jax.vjp(forward, xf, brain_float_kind, cf, unshifted_strides, log_decay_rates, stride_shift, bypass_coefficients)
    grads = backward(result_cotangent.astype(jnp.float32))
    return (core.astype(jnp.bfloat16), grads[0].astype(jnp.bfloat16), grads[1], grads[2], grads[3], grads[4], grads[5], grads[6])
```

```python
import functools

import jax
import jax.numpy as jnp
from jax import lax
from jax.experimental import pallas as pl
from jax.experimental.pallas import tpu as pltpu
from jax.sharding import PartitionSpec as P

MESH = pl.DeviceIdType.MESH
F32, BF16 = jnp.float32, jnp.bfloat16

TOKENS = 128
HEADS = 64
WIDTH = 32
ENTRIES = 128
ROWS = HEADS * WIDTH
HALF = ROWS // 2
GROUP = 8
GROUP_ROWS = GROUP * WIDTH
GROUPS = HEADS // GROUP
CHIPS = 16
PIECE = HALF // CHIPS
SPLIT = (4, 6)


def split(value):
    high = value.astype(BF16)
    return high, (value - high.astype(F32)).astype(BF16)


def mul(a, b):
    return jnp.dot(a, b, preferred_element_type=F32)


def mul_nt(a, b):
    return lax.dot_general(a, b, (((1,), (1,)), ((), ())), preferred_element_type=F32)


def spread(rows, width=WIDTH):
    count = rows.shape[0]
    parts = [jnp.broadcast_to(rows[k : k + 1, :], (width, rows.shape[1])) for k in range(count)]
    return jnp.concatenate(parts, axis=0)


def folded(value, count):
    return jnp.sum(value.reshape(count, WIDTH, value.shape[1]), axis=1)


def lane_sums(value, reverse):
    lanes = lax.broadcasted_iota(jnp.int32, value.shape, 1)
    size = value.shape[1]
    shift = 1
    while shift < size:
        if reverse:
            moved = jnp.where(lanes < size - shift, pltpu.roll(value, size - shift, 1), 0.0)
        else:
            moved = jnp.where(lanes >= shift, pltpu.roll(value, shift, 1), 0.0)
        value = value + moved
        shift *= 2
    return value


def kernel(
    x_ref, b_ref, c_ref, raw_ref, rate_ref, bias_ref, skip_ref, g_ref,
    y_out, dx_out, db_out, dc_out, dt_out, rate_out, bias_out, skip_out,
    xt, gt, gram_t, par_recv, cum_s, step_s, tail_s, grow_s, skip_s, cum_col, step_col,
    tx_hi, tx_lo, eg_hi, eg_lo, txn_hi, txn_lo, egn_hi, egn_lo,
    ends_own, ends_other, state, grad, state_other, grad_other,
    tot_f, tot_b, got_f, got_b, pre_f, pre_b, in_f, in_b, back_f, back_b, carried, later,
    y_t, d_t, dgram_t, u_s, v_s, sk_s, share, share_got, total, total_got,
    par_ss, par_rs, pair_ss, pair_rs, f1_ss, f1_rs, b1_ss, b1_rs, f2_ss, f2_rs, b2_ss, b2_rs,
    back_ss, back_rs, share_ss, share_rs, total_ss, total_rs,
):
    me = lax.axis_index("ctx")
    dp = lax.axis_index("dp")
    n_dp = lax.axis_size("dp")
    n_ctx = lax.axis_size("ctx")
    core = lax.rem(me, 2)
    chip = me // 2
    partner = chip * 2 + 1 - core
    first = core == 0

    def to(src, dst, ss, rs, where):
        return pltpu.make_async_remote_copy(src, dst, ss, rs, device_id=where, device_id_type=MESH)

    barrier = pltpu.get_barrier_semaphore()
    for k in range(1, n_dp):
        pl.semaphore_signal(barrier, 1, device_id={"dp": lax.rem(dp + k, n_dp)}, device_id_type=MESH)
    for k in range(1, n_ctx):
        pl.semaphore_signal(barrier, 1, device_id={"ctx": lax.rem(me + k, n_ctx)}, device_id_type=MESH)

    lanes8 = lax.broadcasted_iota(jnp.int32, (8, 128), 1)
    rows8 = lax.broadcasted_iota(jnp.int32, (8, 128), 0)
    tile = jnp.zeros((8, 128), F32)
    for row, ref in enumerate((rate_ref, bias_ref, skip_ref)):
        for j in range(8):
            here = jnp.logical_and(rows8 == row, lanes8 == dp * 8 + j)
            tile = jnp.where(here, ref[j], tile)
    par_recv[dp] = tile

    for k in range(GROUPS):
        at = slice(k * GROUP_ROWS, (k + 1) * GROUP_ROWS)
        xt[at, :] = jnp.transpose(x_ref[:, at].astype(F32)).astype(BF16)
        gt[at, :] = jnp.transpose(g_ref[:, at].astype(F32)).astype(BF16)
    gram_t[...] = mul_nt(b_ref[...], c_ref[...])

    pl.semaphore_wait(barrier, n_dp + n_ctx - 2)

    sends = []
    for k in range(1, n_dp):
        copy = to(par_recv.at[dp], par_recv.at[dp], par_ss.at[k], par_rs.at[k], {"dp": lax.rem(dp + k, n_dp)})
        copy.start()
        sends.append(copy)
    for copy in sends:
        copy.wait()

    params = par_recv[0]
    for k in range(1, n_dp):
        params = params + par_recv[k]
    columns = jnp.transpose(jnp.concatenate([params] * 16, axis=0))[:HEADS, :]
    square = (HEADS, 128)
    rate = jnp.broadcast_to(columns[:, 0:1], square)
    bias = jnp.broadcast_to(columns[:, 1:2], square)
    skip_s[...] = jnp.broadcast_to(columns[:, 2:3], square)
    z = raw_ref[...] + bias
    step = jnp.maximum(z, 0.0) + jnp.log1p(jnp.exp(-jnp.abs(z)))
    cum = lane_sums(-jnp.exp(rate) * step, False)
    last = jnp.broadcast_to(cum[:, 127:128], square)
    cum_s[...] = cum
    step_s[...] = step
    tail_s[...] = jnp.exp(last - cum) * step
    grow_s[...] = jnp.exp(cum)
    ends_own[...] = jnp.exp(last)

    def states(g):
        rows = pl.ds(pl.multiple_of(g * GROUP_ROWS, GROUP_ROWS), GROUP_ROWS)
        heads = pl.ds(pl.multiple_of(g * GROUP, GROUP), GROUP)
        hi, lo = split(xt[rows, :].astype(F32) * spread(tail_s[heads, :]))
        tx_hi[rows, :] = hi
        tx_lo[rows, :] = lo
        state[rows, :] = mul(hi, b_ref[...]) + mul(lo, b_ref[...])

    def grads(g):
        rows = pl.ds(pl.multiple_of(g * GROUP_ROWS, GROUP_ROWS), GROUP_ROWS)
        heads = pl.ds(pl.multiple_of(g * GROUP, GROUP), GROUP)
        hi, lo = split(gt[rows, :].astype(F32) * spread(grow_s[heads, :]))
        eg_hi[rows, :] = hi
        eg_lo[rows, :] = lo
        grad[rows, :] = mul(hi, c_ref[...]) + mul(lo, c_ref[...])

    mine = pl.ds(pl.multiple_of(core * HALF, HALF), HALF)
    theirs = pl.ds(pl.multiple_of((1 - core) * HALF, HALF), HALF)
    there = {"ctx": partner}
    half_groups = GROUPS // 2
    for k in range(half_groups):
        states((1 - core) * half_groups + k)
    pair = [
        to(ends_own, ends_other, pair_ss.at[0], pair_rs.at[0], there),
        to(state.at[theirs], state_other, pair_ss.at[1], pair_rs.at[1], there),
        to(grad.at[theirs], grad_other, pair_ss.at[2], pair_rs.at[2], there),
    ]
    pair[0].start()
    pair[1].start()
    for k in range(half_groups):
        grads((1 - core) * half_groups + k)
    pair[2].start()
    for k in range(half_groups):
        states(core * half_groups + k)
    for k in range(half_groups):
        grads(core * half_groups + k)

    base = core * (HEADS // 2)

    def row_of(ref, head):
        return jnp.broadcast_to(ref[pl.ds(head, 1), :], (WIDTH, 128))

    def two(ref, r):
        return jnp.concatenate([row_of(ref, base + 2 * r), row_of(ref, base + 2 * r + 1)], axis=0)

    pair[0].wait()
    pair[1].wait()
    for r in range(CHIPS):
        rows = pl.ds(pl.multiple_of(core * HALF + r * PIECE, PIECE), PIECE)
        e_own, e_other = two(ends_own, r), two(ends_other, r)
        own, other = state[rows, :], state_other[r * PIECE : (r + 1) * PIECE, :]
        tot_f[r, 0:PIECE, :] = jnp.where(first, e_other * own + other, own + e_own * other)
        decay = jnp.concatenate(
            [ends_own[pl.ds(base + 2 * r + k, 1), :] * ends_other[pl.ds(base + 2 * r + k, 1), :] for k in range(2)] * 4, axis=0
        )
        tot_f[r, PIECE : PIECE + 8, :] = decay
    got_f[chip] = tot_f[chip]

    def chip_of(k):
        return lax.rem(chip + k, CHIPS)

    def chip_id(k):
        return {"ctx": chip_of(k) * 2 + core}

    f1 = [to(tot_f.at[chip_of(k)], got_f.at[chip], f1_ss.at[k], f1_rs.at[k], chip_id(k)) for k in range(1, CHIPS)]
    for copy in f1:
        copy.start()

    pair[2].wait()
    for r in range(CHIPS):
        rows = pl.ds(pl.multiple_of(core * HALF + r * PIECE, PIECE), PIECE)
        e_own, e_other = two(ends_own, r), two(ends_other, r)
        own, other = grad[rows, :], grad_other[r * PIECE : (r + 1) * PIECE, :]
        tot_b[r] = jnp.where(first, own + e_own * other, e_other * own + other)
    got_b[chip] = tot_b[chip]
    b1 = [to(tot_b.at[chip_of(k)], got_b.at[chip], b1_ss.at[k], b1_rs.at[k], chip_id(k)) for k in range(1, CHIPS)]
    for copy in b1:
        copy.start()

    def padded(value):
        return jnp.transpose(jnp.concatenate([value, value], axis=0))

    cum_t, step_t = padded(cum_s[...]), padded(step_s[...])
    for k in range(GROUPS):
        cum_col[k] = cum_t[:, k * GROUP : (k + 1) * GROUP]
        step_col[k] = step_t[:, k * GROUP : (k + 1) * GROUP]
    dgram_t[...] = jnp.zeros_like(dgram_t)

    def within(g, _):
        rows = pl.ds(pl.multiple_of(g * GROUP_ROWS, GROUP_ROWS), GROUP_ROWS)
        heads = pl.ds(pl.multiple_of(g * GROUP, GROUP), GROUP)
        cum8, cumc, stepc = cum_s[heads, :], cum_col[g], step_col[g]
        xt8, gt8 = xt[rows, :], gt[rows, :]
        above = lax.broadcasted_iota(jnp.int32, (TOKENS, TOKENS), 0) <= lax.broadcasted_iota(
            jnp.int32, (TOKENS, TOKENS), 1
        )
        gram = gram_t[...]
        acc = dgram_t[...]
        none = jnp.zeros((WIDTH, TOKENS), BF16)
        for quad in range(2):
            xq = x_ref[:, pl.ds(pl.multiple_of(g * GROUP_ROWS + quad * 128, 128), 128)]
            for j in range(4):
                k = quad * 4 + j
                at = slice(k * WIDTH, (k + 1) * WIDTH)
                g_rows = gt8[at, :]
                weights_g = jnp.concatenate([g_rows if i == j else none for i in range(4)], axis=0)
                dw = mul(xq, weights_g)
                diff = jnp.broadcast_to(cum8[k : k + 1, :], (TOKENS, TOKENS)) - jnp.broadcast_to(
                    cumc[:, k : k + 1], (TOKENS, TOKENS)
                )
                seg = jnp.exp(jnp.where(above, diff, -1e30))
                factor = seg * jnp.broadcast_to(stepc[:, k : k + 1], (TOKENS, TOKENS))
                acc = acc + dw * factor
                hi, lo = split(gram * factor)
                inner = mul(xt8[at, :], hi) + mul(xt8[at, :], lo)
                back = mul_nt(g_rows, hi) + mul_nt(g_rows, lo)
                out = pl.ds(pl.multiple_of(g * GROUP_ROWS + k * WIDTH, WIDTH), WIDTH)
                y_t[out, :] = inner
                d_t[out, :] = back
        dgram_t[...] = acc
        sk_s[heads, :] = folded(xt8.astype(F32) * gt8.astype(F32), GROUP)
        return 0

    lax.fori_loop(0, SPLIT[0], within, 0)

    for copy in f1:
        copy.wait()
    run = jnp.zeros((PIECE, 128), F32)
    for q in range(CHIPS):
        pre_f[q] = run
        decay = jnp.concatenate(
            [jnp.broadcast_to(got_f[q, PIECE + k : PIECE + k + 1, :], (WIDTH, 128)) for k in range(2)], axis=0
        )
        run = decay * run + got_f[q, 0:PIECE, :]
    in_f[pl.ds(pl.multiple_of(chip * PIECE, PIECE), PIECE), :] = pre_f[chip]
    spot = pl.ds(pl.multiple_of(chip * PIECE, PIECE), PIECE)
    f2 = [to(pre_f.at[chip_of(k)], in_f.at[spot], f2_ss.at[k], f2_rs.at[k], chip_id(k)) for k in range(1, CHIPS)]
    for copy in f2:
        copy.start()

    lax.fori_loop(SPLIT[0], SPLIT[1], within, 0)

    for copy in b1:
        copy.wait()
    run = jnp.zeros((PIECE, 128), F32)
    for q in reversed(range(CHIPS)):
        pre_b[q] = run
        decay = jnp.concatenate(
            [jnp.broadcast_to(got_f[q, PIECE + k : PIECE + k + 1, :], (WIDTH, 128)) for k in range(2)], axis=0
        )
        run = decay * run + got_b[q]
    in_b[pl.ds(pl.multiple_of(chip * PIECE, PIECE), PIECE), :] = pre_b[chip]
    b2 = [to(pre_b.at[chip_of(k)], in_b.at[spot], b2_ss.at[k], b2_rs.at[k], chip_id(k)) for k in range(1, CHIPS)]
    for copy in b2:
        copy.start()

    lax.fori_loop(SPLIT[1], GROUPS, within, 0)

    def turn(k, _):
        rows = pl.ds(pl.multiple_of(k * 128, 128), 128)
        for src, dst in ((tx_hi, txn_hi), (tx_lo, txn_lo), (eg_hi, egn_hi), (eg_lo, egn_lo)):
            dst[:, rows] = jnp.transpose(src[rows, :].astype(F32)).astype(BF16)
        return 0

    lax.fori_loop(0, ROWS // 128, turn, 0)

    for copy in f2:
        copy.wait()
    for r in range(CHIPS):
        at = slice(r * PIECE, (r + 1) * PIECE)
        rows = pl.ds(pl.multiple_of(core * HALF + r * PIECE, PIECE), PIECE)
        e_own, e_other = two(ends_own, r), two(ends_other, r)
        chips = in_f[at, :]
        carried[rows, :] = jnp.where(first, chips, e_other * chips + state_other[at, :])
        back_f[at, :] = jnp.where(first, e_own * chips + state[rows, :], chips)
    back = [
        to(back_f, carried.at[mine], back_ss.at[0], back_rs.at[0], there),
        to(back_b, later.at[mine], back_ss.at[1], back_rs.at[1], there),
    ]
    back[0].start()
    for copy in b2:
        copy.wait()
    for r in range(CHIPS):
        at = slice(r * PIECE, (r + 1) * PIECE)
        rows = pl.ds(pl.multiple_of(core * HALF + r * PIECE, PIECE), PIECE)
        e_own, e_other = two(ends_own, r), two(ends_other, r)
        chips = in_b[at, :]
        later[rows, :] = jnp.where(first, e_other * chips + grad_other[at, :], chips)
        back_b[at, :] = jnp.where(first, chips, e_own * chips + grad[rows, :])
    back[1].start()
    back[0].wait()
    back[1].wait()

    db_out[...] = jnp.zeros_like(db_out)
    dc_out[...] = jnp.zeros_like(dc_out)

    def after(g, end):
        rows = pl.ds(pl.multiple_of(g * GROUP_ROWS, GROUP_ROWS), GROUP_ROWS)
        heads = pl.ds(pl.multiple_of(g * GROUP, GROUP), GROUP)
        a, l = carried[rows, :], later[rows, :]
        a_hi, a_lo = split(a)
        l_hi, l_lo = split(l)
        readout = mul_nt(a_hi, c_ref[...]) + mul_nt(a_lo, c_ref[...])
        q_part = mul_nt(l_hi, b_ref[...]) + mul_nt(l_lo, b_ref[...])
        x8, g8 = xt[rows, :].astype(F32), gt[rows, :].astype(F32)
        y0 = y_t[rows, :] + spread(grow_s[heads, :]) * readout
        tq = spread(tail_s[heads, :]) * q_part
        d0 = d_t[rows, :] + tq
        u_s[heads, :] = folded(g8 * y0, GROUP)
        v_s[heads, :] = folded(x8 * d0, GROUP)
        from_tail = folded(x8 * tq, GROUP)
        cross = folded(a * l, GROUP)
        ends = ends_own[heads, :]
        extra = jnp.sum(from_tail + ends * cross, axis=1, keepdims=True)
        lanes = lax.broadcasted_iota(jnp.int32, (GROUP, 128), 1)
        u_s[heads, :] += jnp.where(lanes == 127, jnp.broadcast_to(extra, (GROUP, 128)), 0.0)
        gains = spread(skip_s[heads, :])
        y_out[:, rows] = jnp.transpose(y0 + gains * x8).astype(BF16)
        dx_out[:, rows] = jnp.transpose(d0 + gains * g8).astype(BF16)
        db_out[...] += mul(txn_hi[:, rows], l_hi) + mul(txn_hi[:, rows], l_lo) + mul(txn_lo[:, rows], l_hi)
        dc_out[...] += mul(egn_hi[:, rows], a_hi) + mul(egn_hi[:, rows], a_lo) + mul(egn_lo[:, rows], a_hi)
        return end

    lax.fori_loop(0, GROUPS, after, 0)

    u, v = u_s[...], v_s[...]
    step = step_s[...]
    rate_gain = jnp.exp(rate)
    dlog = lane_sums(u - v, True)
    dstep = v / step - rate_gain * dlog
    draw = dstep / (1.0 + jnp.exp(-z))
    dt_out[...] = draw
    rate_sum = jnp.sum(dlog * (-rate_gain * step), axis=1, keepdims=True)
    bias_sum = jnp.sum(draw, axis=1, keepdims=True)
    skip_sum = jnp.sum(sk_s[...], axis=1, keepdims=True)
    lanes = lax.broadcasted_iota(jnp.int32, square, 1)
    share[...] = jnp.where(lanes == 0, rate_sum, jnp.where(lanes == 1, bias_sum, jnp.where(lanes == 2, skip_sum, 0.0)))
    own8 = pl.ds(pl.multiple_of(dp * 8, 8), 8)
    share_got[dp] = share[own8, :]
    sends = []
    for k in range(1, n_dp):
        peer = lax.rem(dp + k, n_dp)
        copy = to(
            share.at[pl.ds(pl.multiple_of(peer * 8, 8), 8)], share_got.at[dp], share_ss.at[k], share_rs.at[k], {"dp": peer}
        )
        copy.start()
        sends.append(copy)

    g_hi, g_lo = split(dgram_t[...])
    db_out[...] += mul(g_hi, c_ref[...]) + mul(g_lo, c_ref[...])
    t_hi, t_lo = split(jnp.transpose(dgram_t[...]))
    dc_out[...] += mul(t_hi, b_ref[...]) + mul(t_lo, b_ref[...])

    for copy in sends:
        copy.wait()
    summed = share_got[0]
    for k in range(1, n_dp):
        summed = summed + share_got[k]
    total[...] = summed
    total_got[me] = summed
    sends = []
    for k in range(1, n_ctx):
        copy = to(total, total_got.at[me], total_ss.at[k], total_rs.at[k], {"ctx": lax.rem(me + k, n_ctx)})
        copy.start()
        sends.append(copy)
    for copy in sends:
        copy.wait()
    summed = total_got[0]
    for k in range(1, n_ctx):
        summed = summed + total_got[k]
    lines = jnp.transpose(jnp.concatenate([summed] * 16, axis=0))
    rate_out[...] = lines[0:1, 0:8]
    bias_out[...] = lines[1:2, 0:8]
    skip_out[...] = lines[2:3, 0:8]


def local(x, b, c, raw, rate, bias, skip, g):
    n_dp, n_ctx = lax.axis_size("dp"), lax.axis_size("ctx")
    vmem = pl.BlockSpec(memory_space=pltpu.VMEM)
    smem = pl.BlockSpec(memory_space=pltpu.SMEM)
    wide = (ROWS, 128)
    half = (HALF, 128)
    small = (HEADS, 128)

    def buf(shape, dtype=F32):
        return pltpu.VMEM(shape, dtype)

    scratch = [
        buf(wide, BF16), buf(wide, BF16), buf((TOKENS, TOKENS)), buf((n_dp, 8, 128)),
        *[buf(small)] * 5, buf((GROUPS, TOKENS, GROUP)), buf((GROUPS, TOKENS, GROUP)),
        *[buf(wide, BF16)] * 4, *[buf((TOKENS, ROWS), BF16)] * 4,
        buf(small), buf(small), buf(wide), buf(wide), buf(half), buf(half),
        buf((CHIPS, PIECE + 8, 128)), buf((CHIPS, PIECE, 128)), buf((CHIPS, PIECE + 8, 128)), buf((CHIPS, PIECE, 128)),
        buf((CHIPS, PIECE, 128)), buf((CHIPS, PIECE, 128)), buf(half), buf(half), buf(half), buf(half), buf(wide), buf(wide),
        buf(wide), buf(wide), buf((TOKENS, TOKENS)), buf(small), buf(small), buf(small),
        buf(small), buf((n_dp, 8, 128)), buf((8, 128)), buf((n_ctx, 8, 128)),
        *[pltpu.SemaphoreType.DMA((n_dp,))] * 2, *[pltpu.SemaphoreType.DMA((3,))] * 2,
        *[pltpu.SemaphoreType.DMA((CHIPS,))] * 8, *[pltpu.SemaphoreType.DMA((2,))] * 2,
        *[pltpu.SemaphoreType.DMA((n_dp,))] * 2, *[pltpu.SemaphoreType.DMA((n_ctx,))] * 2,
    ]
    shapes = [
        jax.ShapeDtypeStruct((TOKENS, ROWS), BF16), jax.ShapeDtypeStruct((TOKENS, ROWS), BF16),
        jax.ShapeDtypeStruct((TOKENS, ENTRIES), F32), jax.ShapeDtypeStruct((TOKENS, ENTRIES), F32),
        jax.ShapeDtypeStruct((HEADS, TOKENS), F32),
        *[jax.ShapeDtypeStruct((1, 8), F32)] * 3,
    ]
    y, dx, db, dc, dt, dr, dbias, dskip = pl.pallas_call(
        kernel,
        out_shape=shapes,
        in_specs=[vmem, vmem, vmem, vmem, smem, smem, smem, vmem],
        out_specs=[vmem] * 8,
        scratch_shapes=scratch,
        compiler_params=pltpu.CompilerParams(collective_id=0, has_side_effects=True, vmem_limit_bytes=48 << 20),
        name="layer",
    )(x[0], b[0], c[0], raw[0], rate, bias, skip, g[0])
    return y[None], dx[None], db[None], dc[None], dt[None], dr.reshape(8), dbias.reshape(8), dskip.reshape(8)


def solution(mesh):
    tokens = P("dp", "ctx", None)
    strides = P("dp", None, "ctx")
    owned = P("dp")
    return jax.shard_map(
        local,
        mesh=mesh,
        in_specs=(tokens, tokens, tokens, strides, owned, owned, owned, tokens),
        out_specs=(tokens, tokens, tokens, tokens, strides, owned, owned, owned),
        check_vma=False,
    )
```

```python
import jax
import jax.numpy as jnp
from jax import lax
from jax.experimental import pallas as pl
from jax.experimental.pallas import tpu as pltpu
from jax.sharding import PartitionSpec as P

MESH = pl.DeviceIdType.MESH
F32, BF16 = jnp.float32, jnp.bfloat16

TOKENS = 128
HEADS = 64
WIDTH = 32
ENTRIES = 128
ROWS = HEADS * WIDTH
HALF = ROWS // 2
GROUP = 8
GROUP_ROWS = GROUP * WIDTH
GROUPS = HEADS // GROUP
CHIPS = 16
PIECE = HALF // CHIPS


def split(value):
    high = value.astype(BF16)
    return high, (value - high.astype(F32)).astype(BF16)


def mul(a, b):
    return jnp.dot(a, b, preferred_element_type=F32)


def mul_nt(a, b):
    return lax.dot_general(a, b, (((1,), (1,)), ((), ())), preferred_element_type=F32)


def spread(rows, width=WIDTH):
    count = rows.shape[0]
    parts = [jnp.broadcast_to(rows[k : k + 1, :], (width, rows.shape[1])) for k in range(count)]
    return jnp.concatenate(parts, axis=0)


def folded(value, count):
    return jnp.sum(value.reshape(count, WIDTH, value.shape[1]), axis=1)


def lane_sums(value, reverse):
    lanes = lax.broadcasted_iota(jnp.int32, value.shape, 1)
    size = value.shape[1]
    shift = 1
    while shift < size:
        if reverse:
            moved = jnp.where(lanes < size - shift, pltpu.roll(value, size - shift, 1), 0.0)
        else:
            moved = jnp.where(lanes >= shift, pltpu.roll(value, shift, 1), 0.0)
        value = value + moved
        shift *= 2
    return value
SPLIT = (1, 3, 5)


def layer(
    x_hbm, b_hbm, c_hbm, raw_hbm, rate_hbm, bias_hbm, skip_hbm, g_hbm,
    y_hbm, dx_hbm, db_hbm, dc_hbm, dt_hbm, total_got,
    y_out, dx_out, db_out, dc_out, dt_out,
    x_ref, b_ref, c_ref, raw_ref, g_ref, rate_ref, bias_ref, skip_ref,
    xt, gt, gram_t, par_recv, cum_s, step_s, tail_s, grow_s, skip_s, cum_col, step_col,
    tx_hi, tx_lo, eg_hi, eg_lo, txn_hi, txn_lo, egn_hi, egn_lo,
    ends_own, ends_other, state, grad, state_other, grad_other,
    tot_f, tot_b, got_f, got_b, pre_f, pre_b, in_f, in_b, back_f, back_b, carried, later,
    y_t, d_t, dgram_t, u_s, v_s, sk_s, share, share_got, total,
    in_sem, out_sem, par_ss, par_rs, pair_ss, pair_rs, f1_ss, f1_rs, b1_ss, b1_rs, f2_ss, f2_rs, b2_ss, b2_rs,
    back_ss, back_rs, share_ss, share_rs, total_ss, total_rs,
):
    me = lax.axis_index("ctx")
    dp = lax.axis_index("dp")
    n_dp = lax.axis_size("dp")
    n_ctx = lax.axis_size("ctx")
    core = lax.rem(me, 2)
    chip = me // 2
    partner = chip * 2 + 1 - core
    first = core == 0

    def to(src, dst, ss, rs, where):
        return pltpu.make_async_remote_copy(src, dst, ss, rs, device_id=where, device_id_type=MESH)

    barrier = pltpu.get_barrier_semaphore()
    for k in range(1, n_dp):
        pl.semaphore_signal(barrier, 1, device_id={"dp": lax.rem(dp + k, n_dp)}, device_id_type=MESH)
    for k in range(1, n_ctx):
        pl.semaphore_signal(barrier, 1, device_id={"ctx": lax.rem(me + k, n_ctx)}, device_id_type=MESH)

    loads = [
        pltpu.make_async_copy(src, dst, in_sem.at[k])
        for k, (src, dst) in enumerate(
            (
                (rate_hbm, rate_ref), (bias_hbm, bias_ref), (skip_hbm, skip_ref), (raw_hbm, raw_ref),
                (x_hbm, x_ref), (b_hbm, b_ref), (g_hbm, g_ref), (c_hbm, c_ref),
            )
        )
    ]
    for copy in loads:
        copy.start()
    for copy in loads[:3]:
        copy.wait()

    lanes8 = lax.broadcasted_iota(jnp.int32, (8, 128), 1)
    rows8 = lax.broadcasted_iota(jnp.int32, (8, 128), 0)
    tile = jnp.zeros((8, 128), F32)
    for row, ref in enumerate((rate_ref, bias_ref, skip_ref)):
        for j in range(8):
            here = jnp.logical_and(rows8 == row, lanes8 == dp * 8 + j)
            tile = jnp.where(here, ref[j], tile)
    par_recv[dp] = tile

    pl.semaphore_wait(barrier, n_dp + n_ctx - 2)

    def to_all(src, dst, ss, rs, axis, size, index):
        for k in range(1, size):
            to(src(k), dst, ss.at[0], rs.at[0], {axis: lax.rem(index + k, size)}).start()

    to_all(lambda k: par_recv.at[dp], par_recv.at[dp], par_ss, par_rs, "dp", n_dp, dp)

    for copy in loads[3:]:
        copy.wait()
    for k in range(GROUPS):
        at = slice(k * GROUP_ROWS, (k + 1) * GROUP_ROWS)
        xt[at, :] = jnp.transpose(x_ref[:, at].astype(F32)).astype(BF16)
        gt[at, :] = jnp.transpose(g_ref[:, at].astype(F32)).astype(BF16)
    gram_t[...] = mul_nt(b_ref[...], c_ref[...])

    seven = pl.ds(0, n_dp - 1)
    to(par_recv.at[seven], par_recv.at[seven], par_ss.at[0], par_rs.at[0], {"dp": dp}).wait()

    params = par_recv[0]
    for k in range(1, n_dp):
        params = params + par_recv[k]
    columns = jnp.transpose(jnp.concatenate([params] * 16, axis=0))[:HEADS, :]
    square = (HEADS, 128)
    rate = jnp.broadcast_to(columns[:, 0:1], square)
    bias = jnp.broadcast_to(columns[:, 1:2], square)
    skip_s[...] = jnp.broadcast_to(columns[:, 2:3], square)
    z = raw_ref[...] + bias
    step = jnp.maximum(z, 0.0) + jnp.log1p(jnp.exp(-jnp.abs(z)))
    cum = lane_sums(-jnp.exp(rate) * step, False)
    last = jnp.broadcast_to(cum[:, 127:128], square)
    cum_s[...] = cum
    step_s[...] = step
    tail_s[...] = jnp.exp(last - cum) * step
    grow_s[...] = jnp.exp(cum)
    ends_own[...] = jnp.exp(last)

    def rows_of(g):
        return pl.ds(pl.multiple_of(g * GROUP_ROWS, GROUP_ROWS), GROUP_ROWS)

    def heads_of(g):
        return pl.ds(pl.multiple_of(g * GROUP, GROUP), GROUP)

    outs = [
        pltpu.make_async_copy(src, dst, out_sem.at[k])
        for k, (src, dst) in enumerate(
            (
                (y_out, y_hbm), (dc_out, dc_hbm), (dt_out, dt_hbm), (dx_out, dx_hbm), (db_out, db_hbm),
                (total, total_got.at[me]),
            )
        )
    ]

    def states(g):
        rows, heads = rows_of(g), heads_of(g)
        hi, lo = split(xt[rows, :].astype(F32) * spread(tail_s[heads, :]))
        tx_hi[rows, :] = hi
        tx_lo[rows, :] = lo
        state[rows, :] = mul(hi, b_ref[...]) + mul(lo, b_ref[...])

    def grads(g):
        rows, heads = rows_of(g), heads_of(g)
        hi, lo = split(gt[rows, :].astype(F32) * spread(grow_s[heads, :]))
        eg_hi[rows, :] = hi
        eg_lo[rows, :] = lo
        grad[rows, :] = mul(hi, c_ref[...]) + mul(lo, c_ref[...])

    mine = pl.ds(pl.multiple_of(core * HALF, HALF), HALF)
    theirs = pl.ds(pl.multiple_of((1 - core) * HALF, HALF), HALF)
    there = {"ctx": partner}
    half_groups = GROUPS // 2
    base = core * (HEADS // 2)

    def row_of(ref, head):
        return jnp.broadcast_to(ref[pl.ds(head, 1), :], (WIDTH, 128))

    def two(ref, r):
        return jnp.concatenate([row_of(ref, base + 2 * r), row_of(ref, base + 2 * r + 1)], axis=0)

    def piece_rows(r):
        return pl.ds(pl.multiple_of(core * HALF + r * PIECE, PIECE), PIECE)

    def chip_of(k):
        return lax.rem(chip + k, CHIPS)

    def chip_id(k):
        return {"ctx": chip_of(k) * 2 + core}

    spot = pl.ds(pl.multiple_of(chip * PIECE, PIECE), PIECE)
    others = pl.ds(0, CHIPS - 1)
    most = pl.ds(0, HALF - PIECE)

    def out_pieces(src, dst, ss, rs):
        for k in range(1, CHIPS):
            to(src.at[chip_of(k)], dst, ss.at[0], rs.at[0], chip_id(k)).start()

    def all_pieces(src, ss, rs):
        return to(src.at[others], src.at[others], ss.at[0], rs.at[0], there)

    ends_pair = to(ends_own, ends_other, pair_ss.at[0], pair_rs.at[0], there)
    state_pair = to(state.at[theirs], state_other, pair_ss.at[1], pair_rs.at[1], there)
    grad_pair = to(grad.at[theirs], grad_other, pair_ss.at[2], pair_rs.at[2], there)
    ends_pair.start()
    for k in range(half_groups):
        states((1 - core) * half_groups + k)
    state_pair.start()
    for k in range(half_groups):
        states(core * half_groups + k)

    ends_pair.wait()
    state_pair.wait()
    for r in range(CHIPS):
        e_own, e_other = two(ends_own, r), two(ends_other, r)
        own, other = state[piece_rows(r), :], state_other[r * PIECE : (r + 1) * PIECE, :]
        tot_f[r, 0:PIECE, :] = jnp.where(first, e_other * own + other, own + e_own * other)
        decay = jnp.concatenate(
            [ends_own[pl.ds(base + 2 * r + k, 1), :] * ends_other[pl.ds(base + 2 * r + k, 1), :] for k in range(2)] * 4, axis=0
        )
        tot_f[r, PIECE : PIECE + 8, :] = decay
    got_f[chip] = tot_f[chip]
    out_pieces(tot_f, got_f.at[chip], f1_ss, f1_rs)

    for k in range(half_groups):
        grads((1 - core) * half_groups + k)
    grad_pair.start()
    for k in range(half_groups):
        grads(core * half_groups + k)

    def padded(value):
        return jnp.transpose(jnp.concatenate([value, value], axis=0))

    cum_t, step_t = padded(cum_s[...]), padded(step_s[...])
    for k in range(GROUPS):
        cum_col[k] = cum_t[:, k * GROUP : (k + 1) * GROUP]
        step_col[k] = step_t[:, k * GROUP : (k + 1) * GROUP]
    dgram_t[...] = jnp.zeros_like(dgram_t)

    def within(g, _):
        rows, heads = rows_of(g), heads_of(g)
        cum8, cumc, stepc = cum_s[heads, :], cum_col[g], step_col[g]
        xt8, gt8 = xt[rows, :], gt[rows, :]
        above = lax.broadcasted_iota(jnp.int32, (TOKENS, TOKENS), 0) <= lax.broadcasted_iota(
            jnp.int32, (TOKENS, TOKENS), 1
        )
        gram = gram_t[...]
        acc = dgram_t[...]
        none = jnp.zeros((WIDTH, TOKENS), BF16)
        for quad in range(2):
            xq = x_ref[:, pl.ds(pl.multiple_of(g * GROUP_ROWS + quad * 128, 128), 128)]
            for j in range(4):
                k = quad * 4 + j
                at = slice(k * WIDTH, (k + 1) * WIDTH)
                g_rows = gt8[at, :]
                weights_g = jnp.concatenate([g_rows if i == j else none for i in range(4)], axis=0)
                dw = mul(xq, weights_g)
                diff = jnp.broadcast_to(cum8[k : k + 1, :], (TOKENS, TOKENS)) - jnp.broadcast_to(
                    cumc[:, k : k + 1], (TOKENS, TOKENS)
                )
                seg = jnp.exp(jnp.where(above, diff, -1e30))
                factor = seg * jnp.broadcast_to(stepc[:, k : k + 1], (TOKENS, TOKENS))
                acc = acc + dw * factor
                hi, lo = split(gram * factor)
                inner = mul(xt8[at, :], hi) + mul(xt8[at, :], lo)
                back = mul_nt(g_rows, hi) + mul_nt(g_rows, lo)
                out = pl.ds(pl.multiple_of(g * GROUP_ROWS + k * WIDTH, WIDTH), WIDTH)
                y_t[out, :] = inner
                d_t[out, :] = back
        dgram_t[...] = acc
        sk_s[heads, :] = folded(xt8.astype(F32) * gt8.astype(F32), GROUP)
        return 0

    def turn_of(pairs):
        def turn(k, _):
            rows = pl.ds(pl.multiple_of(k * 128, 128), 128)
            for src, dst in pairs:
                dst[:, rows] = jnp.transpose(src[rows, :].astype(F32)).astype(BF16)
            return 0

        lax.fori_loop(0, ROWS // 128, turn, 0)

    grad_pair.wait()
    for r in range(CHIPS):
        e_own, e_other = two(ends_own, r), two(ends_other, r)
        own, other = grad[piece_rows(r), :], grad_other[r * PIECE : (r + 1) * PIECE, :]
        tot_b[r] = jnp.where(first, own + e_own * other, e_other * own + other)
    got_b[chip] = tot_b[chip]
    lax.fori_loop(0, SPLIT[0], within, 0)
    f1_all = all_pieces(tot_f, f1_ss, f1_rs)
    f1_all.wait_send()
    out_pieces(tot_b, got_b.at[chip], b1_ss, b1_rs)

    lax.fori_loop(SPLIT[0], SPLIT[1], within, 0)

    def decay_of(q):
        return jnp.concatenate(
            [jnp.broadcast_to(got_f[q, PIECE + k : PIECE + k + 1, :], (WIDTH, 128)) for k in range(2)], axis=0
        )

    f1_all.wait_recv()
    run = jnp.zeros((PIECE, 128), F32)
    for q in range(CHIPS):
        pre_f[q] = run
        run = decay_of(q) * run + got_f[q, 0:PIECE, :]
    in_f[spot, :] = pre_f[chip]
    b1_all = all_pieces(tot_b, b1_ss, b1_rs)
    b1_all.wait_send()
    out_pieces(pre_f, in_f.at[spot], f2_ss, f2_rs)

    lax.fori_loop(SPLIT[1], SPLIT[2], within, 0)

    b1_all.wait_recv()
    run = jnp.zeros((PIECE, 128), F32)
    for q in reversed(range(CHIPS)):
        pre_b[q] = run
        run = decay_of(q) * run + got_b[q]
    in_b[spot, :] = pre_b[chip]
    all_pieces(pre_f, f2_ss, f2_rs).wait_send()
    out_pieces(pre_b, in_b.at[spot], b2_ss, b2_rs)

    lax.fori_loop(SPLIT[2], GROUPS, within, 0)

    back_f_pair = to(back_f, carried.at[mine], back_ss.at[0], back_rs.at[0], there)
    back_b_pair = to(back_b, later.at[mine], back_ss.at[1], back_rs.at[1], there)
    to(in_f.at[most], in_f.at[most], f2_ss.at[0], f2_rs.at[0], there).wait_recv()
    for r in range(CHIPS):
        at = slice(r * PIECE, (r + 1) * PIECE)
        e_own, e_other = two(ends_own, r), two(ends_other, r)
        chips = in_f[at, :]
        carried[piece_rows(r), :] = jnp.where(first, chips, e_other * chips + state_other[at, :])
        back_f[at, :] = jnp.where(first, e_own * chips + state[piece_rows(r), :], chips)
    back_f_pair.start()
    turn_of(((eg_hi, egn_hi), (eg_lo, egn_lo)))
    back_f_pair.wait()

    dc_out[...] = jnp.zeros_like(dc_out)
    db_out[...] = jnp.zeros_like(db_out)

    def after_f(g, _):
        rows, heads = rows_of(g), heads_of(g)
        a_hi, a_lo = split(carried[rows, :])
        readout = mul_nt(a_hi, c_ref[...]) + mul_nt(a_lo, c_ref[...])
        x8, g8 = xt[rows, :].astype(F32), gt[rows, :].astype(F32)
        y0 = y_t[rows, :] + spread(grow_s[heads, :]) * readout
        u_s[heads, :] = folded(g8 * y0, GROUP)
        y_out[:, rows] = jnp.transpose(y0 + spread(skip_s[heads, :]) * x8).astype(BF16)
        dc_out[...] += mul(egn_hi[:, rows], a_hi) + mul(egn_hi[:, rows], a_lo) + mul(egn_lo[:, rows], a_hi)
        return 0

    lax.fori_loop(0, GROUPS, after_f, 0)
    turn_of(((tx_hi, txn_hi), (tx_lo, txn_lo)))
    g_hi, g_lo = split(dgram_t[...])
    db_out[...] += mul(g_hi, c_ref[...]) + mul(g_lo, c_ref[...])
    t_hi, t_lo = split(jnp.transpose(dgram_t[...]))
    dc_out[...] += mul(t_hi, b_ref[...]) + mul(t_lo, b_ref[...])
    outs[0].start()
    outs[1].start()

    to(in_b.at[most], in_b.at[most], b2_ss.at[0], b2_rs.at[0], there).wait_recv()
    for r in range(CHIPS):
        at = slice(r * PIECE, (r + 1) * PIECE)
        e_own, e_other = two(ends_own, r), two(ends_other, r)
        chips = in_b[at, :]
        later[piece_rows(r), :] = jnp.where(first, e_other * chips + grad_other[at, :], chips)
        back_b[at, :] = jnp.where(first, chips, e_own * chips + grad[piece_rows(r), :])
    back_b_pair.start()

    def after_b(g, _):
        rows, heads = rows_of(g), heads_of(g)
        l = later[rows, :]
        l_hi, l_lo = split(l)
        tq = spread(tail_s[heads, :]) * (mul_nt(l_hi, b_ref[...]) + mul_nt(l_lo, b_ref[...]))
        x8 = xt[rows, :].astype(F32)
        d0 = d_t[rows, :] + tq
        d_t[rows, :] = d0
        v_s[heads, :] = folded(x8 * d0, GROUP)
        extra = folded(x8 * tq, GROUP) + ends_own[heads, :] * folded(carried[rows, :] * l, GROUP)
        extra = jnp.broadcast_to(jnp.sum(extra, axis=1, keepdims=True), (GROUP, 128))
        lanes = lax.broadcasted_iota(jnp.int32, (GROUP, 128), 1)
        u_s[heads, :] += jnp.where(lanes == 127, extra, 0.0)
        return 0

    lax.fori_loop(core * half_groups, (core + 1) * half_groups, after_b, 0)
    back_b_pair.wait()
    lax.fori_loop((1 - core) * half_groups, (2 - core) * half_groups, after_b, 0)

    u, v = u_s[...], v_s[...]
    step = step_s[...]
    rate_gain = jnp.exp(rate)
    dlog = lane_sums(u - v, True)
    dstep = v / step - rate_gain * dlog
    draw = dstep / (1.0 + jnp.exp(-z))
    dt_out[...] = draw
    outs[2].start()
    rate_sum = jnp.sum(dlog * (-rate_gain * step), axis=1, keepdims=True)
    bias_sum = jnp.sum(draw, axis=1, keepdims=True)
    skip_sum = jnp.sum(sk_s[...], axis=1, keepdims=True)
    lanes = lax.broadcasted_iota(jnp.int32, square, 1)
    share[...] = jnp.where(lanes == 0, rate_sum, jnp.where(lanes == 1, bias_sum, jnp.where(lanes == 2, skip_sum, 0.0)))

    def eight(d):
        return pl.ds(pl.multiple_of(d * 8, 8), 8)

    share_got[dp] = share[eight(dp), :]
    to_all(lambda k: share.at[eight(lax.rem(dp + k, n_dp))], share_got.at[dp], share_ss, share_rs, "dp", n_dp, dp)

    def finish(g, _):
        rows, heads = rows_of(g), heads_of(g)
        g8 = gt[rows, :].astype(F32)
        dx_out[:, rows] = jnp.transpose(d_t[rows, :] + spread(skip_s[heads, :]) * g8).astype(BF16)
        l_hi, l_lo = split(later[rows, :])
        db_out[...] += mul(txn_hi[:, rows], l_hi) + mul(txn_hi[:, rows], l_lo) + mul(txn_lo[:, rows], l_hi)
        return 0

    lax.fori_loop(0, GROUPS, finish, 0)
    outs[3].start()
    outs[4].start()

    to(share_got.at[seven], share_got.at[seven], share_ss.at[0], share_rs.at[0], {"dp": dp}).wait()
    summed = share_got[0]
    for k in range(1, n_dp):
        summed = summed + share_got[k]
    total[...] = summed
    outs[5].start()
    to_all(lambda k: total, total_got.at[me], total_ss, total_rs, "ctx", n_ctx, me)
    all_pieces(pre_b, b2_ss, b2_rs).wait_send()
    for copy in outs:
        copy.wait()
    last31 = pl.ds(0, n_ctx - 1)
    to(total_got.at[last31], total_got.at[last31], total_ss.at[0], total_rs.at[0], {"ctx": me}).wait()


def write(*refs):
    sources, targets, buffers, lines, in_sem, out_sem = refs[:6], refs[6:14], refs[14:20], refs[20], refs[21], refs[22]
    loads = [pltpu.make_async_copy(src, dst, in_sem.at[k]) for k, (src, dst) in enumerate(zip(sources, buffers))]
    loads = loads[5:] + loads[:5]
    for copy in loads:
        copy.start()
    kept = [*buffers[:5], lines.at[0], lines.at[1], lines.at[2]]
    stores = [pltpu.make_async_copy(src, dst, out_sem.at[k]) for k, (src, dst) in enumerate(zip(kept, targets))]
    loads[0].wait()
    totals = buffers[5]
    summed = totals[0]
    for k in range(1, totals.shape[0]):
        summed = summed + totals[k]
    turned = jnp.transpose(jnp.concatenate([summed] * 16, axis=0))
    for k in range(3):
        lines[k] = turned[k : k + 1, 0:8]
        stores[5 + k].start()
    for k in range(5):
        loads[1 + k].wait()
        stores[k].start()
    for copy in stores:
        copy.wait()


def local(x, b, c, raw, rate, bias, skip, g):
    n_dp, n_ctx = lax.axis_size("dp"), lax.axis_size("ctx")
    vmem = pl.BlockSpec(memory_space=pltpu.VMEM)
    hbm = pl.BlockSpec(memory_space=pltpu.HBM)
    wide = (ROWS, 128)
    half = (HALF, 128)
    small = (HEADS, 128)
    piece = (CHIPS, PIECE, 128)
    longer = (CHIPS, PIECE + 8, 128)

    def buf(shape, dtype=F32):
        return pltpu.VMEM(shape, dtype)

    def sems(count):
        return pltpu.SemaphoreType.DMA((count,))

    landing = [
        buf((TOKENS, ROWS), BF16), buf((TOKENS, ROWS), BF16), buf((TOKENS, ENTRIES)), buf((TOKENS, ENTRIES)), buf(small),
        buf((n_ctx, 8, 128)),
    ]
    scratch = [
        *landing[:5],
        buf((TOKENS, ROWS), BF16), buf((TOKENS, ENTRIES), BF16), buf((TOKENS, ENTRIES), BF16), buf(small),
        buf((TOKENS, ROWS), BF16), *[pltpu.SMEM((8,), F32)] * 3,
        buf(wide, BF16), buf(wide, BF16), buf((TOKENS, TOKENS)), buf((n_dp, 8, 128)),
        *[buf(small)] * 5, buf((GROUPS, TOKENS, GROUP)), buf((GROUPS, TOKENS, GROUP)),
        *[buf(wide, BF16)] * 4, *[buf((TOKENS, ROWS), BF16)] * 4,
        buf(small), buf(small), buf(wide), buf(wide), buf(half), buf(half),
        buf(longer), buf(piece), buf(longer), buf(piece),
        buf(piece), buf(piece), buf(half), buf(half), buf(half), buf(half), buf(wide), buf(wide),
        buf(wide), buf(wide), buf((TOKENS, TOKENS)), buf(small), buf(small), buf(small),
        buf(small), buf((n_dp, 8, 128)), buf((8, 128)),
        sems(8), sems(6), sems(1), sems(1), sems(3), sems(3), *[sems(1)] * 8, sems(2), sems(2), *[sems(1)] * 4,
    ]
    wide_out = jax.ShapeDtypeStruct((TOKENS, ROWS), BF16)
    square_out = jax.ShapeDtypeStruct((TOKENS, ENTRIES), F32)
    dt_shape = jax.ShapeDtypeStruct((HEADS, TOKENS), F32)
    shapes = [wide_out, wide_out, square_out, square_out, dt_shape]
    results = pl.pallas_call(
        layer,
        out_shape=[*shapes, jax.ShapeDtypeStruct((n_ctx, 8, 128), F32)],
        in_specs=[hbm] * 8,
        out_specs=[hbm] * 6,
        scratch_shapes=scratch,
        compiler_params=pltpu.CompilerParams(collective_id=0, has_side_effects=True, vmem_limit_bytes=60 << 20),
        name="layer",
    )(x[0], b[0], c[0], raw[0], rate, bias, skip, g[0])
    y, dx, db, dc, dt, dr, dbias, dskip = pl.pallas_call(
        write,
        out_shape=[*shapes, *[jax.ShapeDtypeStruct((1, 8), F32)] * 3],
        in_specs=[hbm] * 6,
        out_specs=[hbm] * 8,
        scratch_shapes=[*landing, buf((3, 1, 8)), sems(6), sems(8)],
        compiler_params=pltpu.CompilerParams(vmem_limit_bytes=60 << 20),
        name="write",
    )(*results)
    return y[None], dx[None], db[None], dc[None], dt[None], dr.reshape(8), dbias.reshape(8), dskip.reshape(8)


def solution(mesh):
    tokens = P("dp", "ctx", None)
    strides = P("dp", None, "ctx")
    owned = P("dp")
    return jax.shard_map(
        local,
        mesh=mesh,
        in_specs=(tokens, tokens, tokens, strides, owned, owned, owned, tokens),
        out_specs=(tokens, tokens, tokens, tokens, strides, owned, owned, owned),
        check_vma=False,
    )
```

```python
import jax
import jax.numpy as jnp
from jax import lax
from jax.experimental import pallas as pl
from jax.experimental.pallas import tpu as pltpu
from jax.sharding import PartitionSpec as P

MESH = pl.DeviceIdType.MESH
F32, BF16 = jnp.float32, jnp.bfloat16

TOKENS = 128
HEADS = 64
WIDTH = 32
ENTRIES = 128
ROWS = HEADS * WIDTH
HALF = ROWS // 2
GROUP = 8
GROUP_ROWS = GROUP * WIDTH
GROUPS = HEADS // GROUP
CHIPS = 16
PIECE = HALF // CHIPS


def split(value):
    high = value.astype(BF16)
    return high, (value - high.astype(F32)).astype(BF16)


def mul(a, b):
    return jnp.dot(a, b, preferred_element_type=F32)


def mul_nt(a, b):
    return lax.dot_general(a, b, (((1,), (1,)), ((), ())), preferred_element_type=F32)


def spread(rows, width=WIDTH):
    count = rows.shape[0]
    parts = [jnp.broadcast_to(rows[k : k + 1, :], (width, rows.shape[1])) for k in range(count)]
    return jnp.concatenate(parts, axis=0)


def folded(value, count):
    return jnp.sum(value.reshape(count, WIDTH, value.shape[1]), axis=1)


def lane_sums(value, reverse):
    lanes = lax.broadcasted_iota(jnp.int32, value.shape, 1)
    size = value.shape[1]
    shift = 1
    while shift < size:
        if reverse:
            moved = jnp.where(lanes < size - shift, pltpu.roll(value, size - shift, 1), 0.0)
        else:
            moved = jnp.where(lanes >= shift, pltpu.roll(value, shift, 1), 0.0)
        value = value + moved
        shift *= 2
    return value
SPLIT = (1, 3, 5)


def layer(
    x_hbm, b_hbm, c_hbm, raw_hbm, rate_hbm, bias_hbm, skip_hbm, g_hbm,
    y_hbm, dx_hbm, db_hbm, dc_hbm, dt_hbm, total_got,
    y_out, dx_out, db_out, dc_out, dt_out,
    x_ref, b_ref, c_ref, raw_ref, g_ref, rate_ref, bias_ref, skip_ref,
    xt, gt, gram_t, par_recv, cum_s, step_s, tail_s, grow_s, skip_s, cum_col, step_col,
    txn_hi, txn_lo, egn_hi, egn_lo, rate_s, bias_s, pack_own, x_own, g_own, pack_other, x_other, g_other, tail_o, grow_o,
    ends_own, ends_other, state, grad, state_other, grad_other,
    tot_f, tot_b, got_f, got_b, pre_f, pre_b, in_f, in_b, back_f, back_b, carried, later,
    y_t, d_t, dgram_t, u_s, v_s, sk_s, share, share_got, total,
    in_sem, out_sem, par_ss, par_rs, pair_ss, pair_rs, f1_ss, f1_rs, b1_ss, b1_rs, f2_ss, f2_rs, b2_ss, b2_rs,
    back_ss, back_rs, share_ss, share_rs, total_ss, total_rs,
):
    me = lax.axis_index("ctx")
    dp = lax.axis_index("dp")
    n_dp = lax.axis_size("dp")
    n_ctx = lax.axis_size("ctx")
    core = lax.rem(me, 2)
    chip = me // 2
    partner = chip * 2 + 1 - core
    first = core == 0

    def to(src, dst, ss, rs, where):
        return pltpu.make_async_remote_copy(src, dst, ss, rs, device_id=where, device_id_type=MESH)

    barrier = pltpu.get_barrier_semaphore()
    for k in range(1, n_dp):
        pl.semaphore_signal(barrier, 1, device_id={"dp": lax.rem(dp + k, n_dp)}, device_id_type=MESH)
    for k in range(1, n_ctx):
        pl.semaphore_signal(barrier, 1, device_id={"ctx": lax.rem(me + k, n_ctx)}, device_id_type=MESH)

    loads = [
        pltpu.make_async_copy(src, dst, in_sem.at[k])
        for k, (src, dst) in enumerate(
            (
                (rate_hbm, rate_ref), (bias_hbm, bias_ref), (skip_hbm, skip_ref), (raw_hbm, raw_ref),
                (x_hbm, x_ref), (b_hbm, b_ref), (g_hbm, g_ref), (c_hbm, c_ref),
            )
        )
    ]
    for copy in loads:
        copy.start()
    for copy in loads[:3]:
        copy.wait()

    lanes8 = lax.broadcasted_iota(jnp.int32, (8, 128), 1)
    rows8 = lax.broadcasted_iota(jnp.int32, (8, 128), 0)
    tile = jnp.zeros((8, 128), F32)
    for row, ref in enumerate((rate_ref, bias_ref, skip_ref)):
        for j in range(8):
            here = jnp.logical_and(rows8 == row, lanes8 == dp * 8 + j)
            tile = jnp.where(here, ref[j], tile)
    par_recv[dp] = tile

    pl.semaphore_wait(barrier, n_dp + n_ctx - 2)

    def to_all(src, dst, ss, rs, axis, size, index):
        for k in range(1, size):
            to(src(k), dst, ss.at[0], rs.at[0], {axis: lax.rem(index + k, size)}).start()

    to_all(lambda k: par_recv.at[dp], par_recv.at[dp], par_ss, par_rs, "dp", n_dp, dp)

    there = {"ctx": partner}
    pack_pair = to(pack_own, pack_other, pair_ss.at[0], pair_rs.at[0], there)
    x_pair = to(x_own, x_other, pair_ss.at[1], pair_rs.at[1], there)
    g_pair = to(g_own, g_other, pair_ss.at[2], pair_rs.at[2], there)
    half_groups = GROUPS // 2
    heads_here = HEADS // 2
    for copy in loads[3:]:
        copy.wait()
    pack_own[0:TOKENS, :] = b_ref[...].astype(F32)
    pack_own[TOKENS : 2 * TOKENS, :] = c_ref[...].astype(F32)
    pack_own[2 * TOKENS :, :] = raw_ref[pl.ds(pl.multiple_of((1 - core) * heads_here, heads_here), heads_here), :]
    pack_pair.start()

    def turned(src, dst, sent, half):
        for k in range(half_groups):
            rows = pl.ds(pl.multiple_of(half * HALF + k * GROUP_ROWS, GROUP_ROWS), GROUP_ROWS)
            value = jnp.transpose(src[:, rows].astype(F32))
            dst[rows, :] = value.astype(BF16)
            if sent is not None:
                sent[k * GROUP_ROWS : (k + 1) * GROUP_ROWS, :] = value

    turned(x_ref, xt, x_own, 1 - core)
    x_pair.start()
    turned(g_ref, gt, g_own, 1 - core)
    g_pair.start()
    turned(x_ref, xt, None, core)
    turned(g_ref, gt, None, core)
    gram_t[...] = mul_nt(b_ref[...], c_ref[...])

    seven = pl.ds(0, n_dp - 1)
    to(par_recv.at[seven], par_recv.at[seven], par_ss.at[0], par_rs.at[0], {"dp": dp}).wait()

    params = par_recv[0]
    for k in range(1, n_dp):
        params = params + par_recv[k]
    columns = jnp.transpose(jnp.concatenate([params] * 16, axis=0))[:HEADS, :]
    square = (HEADS, 128)
    rate = jnp.broadcast_to(columns[:, 0:1], square)
    bias = jnp.broadcast_to(columns[:, 1:2], square)
    skip_s[...] = jnp.broadcast_to(columns[:, 2:3], square)
    rate_s[...] = rate
    bias_s[...] = bias

    def steps_of(raw, rate, bias):
        z = raw + bias
        step = jnp.maximum(z, 0.0) + jnp.log1p(jnp.exp(-jnp.abs(z)))
        cum = lane_sums(-jnp.exp(rate) * step, False)
        return z, step, cum, jnp.broadcast_to(cum[:, 127:128], cum.shape)

    z, step, cum, last = steps_of(raw_ref[...], rate, bias)
    cum_s[...] = cum
    step_s[...] = step
    tail_s[...] = jnp.exp(last - cum) * step
    grow_s[...] = jnp.exp(cum)
    ends_own[...] = jnp.exp(last)
    here = pl.ds(pl.multiple_of(core * heads_here, heads_here), heads_here)
    pack_pair.wait()
    _, step_o, cum_o, last_o = steps_of(pack_other[2 * TOKENS :, :], rate_s[here, :], bias_s[here, :])
    tail_o[...] = jnp.exp(last_o - cum_o) * step_o
    grow_o[...] = jnp.exp(cum_o)
    ends_other[...] = jnp.exp(last_o)
    b_other = pack_other[0:TOKENS, :].astype(BF16)
    c_other = pack_other[TOKENS : 2 * TOKENS, :].astype(BF16)

    def rows_of(g):
        return pl.ds(pl.multiple_of(g * GROUP_ROWS, GROUP_ROWS), GROUP_ROWS)

    def heads_of(g):
        return pl.ds(pl.multiple_of(g * GROUP, GROUP), GROUP)

    outs = [
        pltpu.make_async_copy(src, dst, out_sem.at[k])
        for k, (src, dst) in enumerate(
            (
                (y_out, y_hbm), (dc_out, dc_hbm), (dt_out, dt_hbm), (dx_out, dx_hbm), (db_out, db_hbm),
                (total, total_got.at[me]),
            )
        )
    ]

    mine = pl.ds(pl.multiple_of(core * HALF, HALF), HALF)
    base = core * (HEADS // 2)

    def row_of(ref, head):
        return jnp.broadcast_to(ref[pl.ds(head, 1), :], (WIDTH, 128))

    def two(ref, r):
        at = base + 2 * r if ref is ends_own else 2 * r
        return jnp.concatenate([row_of(ref, at), row_of(ref, at + 1)], axis=0)

    def piece_rows(r):
        return pl.ds(pl.multiple_of(core * HALF + r * PIECE, PIECE), PIECE)

    def chip_of(k):
        return lax.rem(chip + k, CHIPS)

    def chip_id(k):
        return {"ctx": chip_of(k) * 2 + core}

    spot = pl.ds(pl.multiple_of(chip * PIECE, PIECE), PIECE)
    others = pl.ds(0, CHIPS - 1)
    most = pl.ds(0, HALF - PIECE)

    def out_pieces(src, dst, ss, rs):
        for k in range(1, CHIPS):
            to(src.at[chip_of(k)], dst, ss.at[0], rs.at[0], chip_id(k)).start()

    def all_pieces(src, ss, rs):
        return to(src.at[others], src.at[others], ss.at[0], rs.at[0], there)

    def product(rows, gains, entries):
        hi, lo = split(rows.astype(F32) * spread(gains))
        return mul(hi, entries) + mul(lo, entries)

    row = chip // 4

    def send(src, dst, ss, rs, g):
        for j in range(4):
            target = g * 4 + lax.rem(chip + j, 4)

            @pl.when(target != chip)
            def _():
                to(src.at[target], dst, ss.at[0], rs.at[0], {"ctx": target * 2 + core}).start()

    def totals_f(k, _):
        g = lax.rem(row + k + 1, 4)
        rows, heads = rows_of(core * half_groups + g), heads_of(core * half_groups + g)
        local_rows, local_heads = rows_of(g), heads_of(g)
        own = product(xt[rows, :], tail_s[heads, :], b_ref[...])
        other = product(x_other[local_rows, :], tail_o[local_heads, :], b_other)
        state[rows, :] = own
        state_other[local_rows, :] = other
        e_own, e_other = ends_own[heads, :], ends_other[local_heads, :]
        both = jnp.where(first, spread(e_other) * own + other, own + spread(e_own) * other)
        decay = e_own * e_other
        for j in range(4):
            tot_f[g * 4 + j, 0:PIECE, :] = both[j * PIECE : (j + 1) * PIECE, :]
            tot_f[g * 4 + j, PIECE : PIECE + 8, :] = jnp.concatenate([decay[2 * j : 2 * j + 2, :]] * 4, axis=0)
        send(tot_f, got_f.at[chip], f1_ss, f1_rs, g)
        return 0

    def totals_b(k, _):
        g = lax.rem(row + k + 1, 4)
        rows, heads = rows_of(core * half_groups + g), heads_of(core * half_groups + g)
        local_rows, local_heads = rows_of(g), heads_of(g)
        own = product(gt[rows, :], grow_s[heads, :], c_ref[...])
        other = product(g_other[local_rows, :], grow_o[local_heads, :], c_other)
        grad[rows, :] = own
        grad_other[local_rows, :] = other
        e_own, e_other = ends_own[heads, :], ends_other[local_heads, :]
        both = jnp.where(first, own + spread(e_own) * other, spread(e_other) * own + other)
        for j in range(4):
            tot_b[g * 4 + j] = both[j * PIECE : (j + 1) * PIECE, :]
        return 0

    x_pair.wait()
    lax.fori_loop(0, half_groups, totals_f, 0)
    got_f[chip] = tot_f[chip]
    g_pair.wait()
    lax.fori_loop(0, half_groups, totals_b, 0)
    got_b[chip] = tot_b[chip]

    def padded(value):
        return jnp.transpose(jnp.concatenate([value, value], axis=0))

    cum_t, step_t = padded(cum_s[...]), padded(step_s[...])
    for k in range(GROUPS):
        cum_col[k] = cum_t[:, k * GROUP : (k + 1) * GROUP]
        step_col[k] = step_t[:, k * GROUP : (k + 1) * GROUP]
    dgram_t[...] = jnp.zeros_like(dgram_t)

    def within(g, _):
        rows, heads = rows_of(g), heads_of(g)
        cum8, cumc, stepc = cum_s[heads, :], cum_col[g], step_col[g]
        xt8, gt8 = xt[rows, :], gt[rows, :]
        above = lax.broadcasted_iota(jnp.int32, (TOKENS, TOKENS), 0) <= lax.broadcasted_iota(
            jnp.int32, (TOKENS, TOKENS), 1
        )
        gram = gram_t[...]
        acc = dgram_t[...]
        none = jnp.zeros((WIDTH, TOKENS), BF16)
        for quad in range(2):
            xq = x_ref[:, pl.ds(pl.multiple_of(g * GROUP_ROWS + quad * 128, 128), 128)]
            for j in range(4):
                k = quad * 4 + j
                at = slice(k * WIDTH, (k + 1) * WIDTH)
                g_rows = gt8[at, :]
                weights_g = jnp.concatenate([g_rows if i == j else none for i in range(4)], axis=0)
                dw = mul(xq, weights_g)
                diff = jnp.broadcast_to(cum8[k : k + 1, :], (TOKENS, TOKENS)) - jnp.broadcast_to(
                    cumc[:, k : k + 1], (TOKENS, TOKENS)
                )
                seg = jnp.exp(jnp.where(above, diff, -1e30))
                factor = seg * jnp.broadcast_to(stepc[:, k : k + 1], (TOKENS, TOKENS))
                acc = acc + dw * factor
                hi, lo = split(gram * factor)
                inner = mul(xt8[at, :], hi) + mul(xt8[at, :], lo)
                back = mul_nt(g_rows, hi) + mul_nt(g_rows, lo)
                out = pl.ds(pl.multiple_of(g * GROUP_ROWS + k * WIDTH, WIDTH), WIDTH)
                y_t[out, :] = inner
                d_t[out, :] = back
        dgram_t[...] = acc
        sk_s[heads, :] = folded(xt8.astype(F32) * gt8.astype(F32), GROUP)
        return 0

    def turn_of(src, gains, hi_out, lo_out):
        def turn(g, _):
            rows, heads = rows_of(g), heads_of(g)
            hi, lo = split(jnp.transpose(src[rows, :].astype(F32) * spread(gains[heads, :])))
            hi_out[:, rows] = hi
            lo_out[:, rows] = lo
            return 0

        lax.fori_loop(0, GROUPS, turn, 0)

    lax.fori_loop(0, SPLIT[0], within, 0)
    f1_all = all_pieces(tot_f, f1_ss, f1_rs)
    f1_all.wait_send()
    out_pieces(tot_b, got_b.at[chip], b1_ss, b1_rs)

    lax.fori_loop(SPLIT[0], SPLIT[1], within, 0)

    def decay_of(q):
        return jnp.concatenate(
            [jnp.broadcast_to(got_f[q, PIECE + k : PIECE + k + 1, :], (WIDTH, 128)) for k in range(2)], axis=0
        )

    f1_all.wait_recv()
    run = jnp.zeros((PIECE, 128), F32)
    for q in range(CHIPS):
        pre_f[q] = run
        run = decay_of(q) * run + got_f[q, 0:PIECE, :]
    in_f[spot, :] = pre_f[chip]
    b1_all = all_pieces(tot_b, b1_ss, b1_rs)
    out_pieces(pre_f, in_f.at[spot], f2_ss, f2_rs)

    lax.fori_loop(SPLIT[1], SPLIT[2], within, 0)

    b1_all.wait_recv()
    run = jnp.zeros((PIECE, 128), F32)
    for q in reversed(range(CHIPS)):
        pre_b[q] = run
        run = decay_of(q) * run + got_b[q]
    in_b[spot, :] = pre_b[chip]
    all_pieces(pre_f, f2_ss, f2_rs).wait_send()
    out_pieces(pre_b, in_b.at[spot], b2_ss, b2_rs)

    lax.fori_loop(SPLIT[2], GROUPS, within, 0)

    back_f_pair = to(back_f, carried.at[mine], back_ss.at[0], back_rs.at[0], there)
    back_b_pair = to(back_b, later.at[mine], back_ss.at[1], back_rs.at[1], there)
    to(in_f.at[most], in_f.at[most], f2_ss.at[0], f2_rs.at[0], there).wait_recv()
    for r in range(CHIPS):
        at = slice(r * PIECE, (r + 1) * PIECE)
        e_own, e_other = two(ends_own, r), two(ends_other, r)
        chips = in_f[at, :]
        carried[piece_rows(r), :] = jnp.where(first, chips, e_other * chips + state_other[at, :])
        back_f[at, :] = jnp.where(first, e_own * chips + state[piece_rows(r), :], chips)
    back_f_pair.start()
    turn_of(gt, grow_s, egn_hi, egn_lo)
    back_f_pair.wait()

    dc_out[...] = jnp.zeros_like(dc_out)
    db_out[...] = jnp.zeros_like(db_out)

    def after_f(g, _):
        rows, heads = rows_of(g), heads_of(g)
        a_hi, a_lo = split(carried[rows, :])
        readout = mul_nt(a_hi, c_ref[...]) + mul_nt(a_lo, c_ref[...])
        x8, g8 = xt[rows, :].astype(F32), gt[rows, :].astype(F32)
        y0 = y_t[rows, :] + spread(grow_s[heads, :]) * readout
        u_s[heads, :] = folded(g8 * y0, GROUP)
        y_out[:, rows] = jnp.transpose(y0 + spread(skip_s[heads, :]) * x8).astype(BF16)
        dc_out[...] += mul(egn_hi[:, rows], a_hi) + mul(egn_hi[:, rows], a_lo) + mul(egn_lo[:, rows], a_hi)
        return 0

    lax.fori_loop(0, GROUPS, after_f, 0)
    turn_of(xt, tail_s, txn_hi, txn_lo)
    g_hi, g_lo = split(dgram_t[...])
    db_out[...] += mul(g_hi, c_ref[...]) + mul(g_lo, c_ref[...])
    t_hi, t_lo = split(jnp.transpose(dgram_t[...]))
    dc_out[...] += mul(t_hi, b_ref[...]) + mul(t_lo, b_ref[...])
    outs[0].start()
    outs[1].start()

    to(in_b.at[most], in_b.at[most], b2_ss.at[0], b2_rs.at[0], there).wait_recv()
    for r in range(CHIPS):
        at = slice(r * PIECE, (r + 1) * PIECE)
        e_own, e_other = two(ends_own, r), two(ends_other, r)
        chips = in_b[at, :]
        later[piece_rows(r), :] = jnp.where(first, e_other * chips + grad_other[at, :], chips)
        back_b[at, :] = jnp.where(first, chips, e_own * chips + grad[piece_rows(r), :])
    back_b_pair.start()

    def after_b(g, _):
        rows, heads = rows_of(g), heads_of(g)
        l = later[rows, :]
        l_hi, l_lo = split(l)
        tq = spread(tail_s[heads, :]) * (mul_nt(l_hi, b_ref[...]) + mul_nt(l_lo, b_ref[...]))
        x8 = xt[rows, :].astype(F32)
        d0 = d_t[rows, :] + tq
        d_t[rows, :] = d0
        v_s[heads, :] = folded(x8 * d0, GROUP)
        extra = folded(x8 * tq, GROUP) + ends_own[heads, :] * folded(carried[rows, :] * l, GROUP)
        extra = jnp.broadcast_to(jnp.sum(extra, axis=1, keepdims=True), (GROUP, 128))
        lanes = lax.broadcasted_iota(jnp.int32, (GROUP, 128), 1)
        u_s[heads, :] += jnp.where(lanes == 127, extra, 0.0)
        return 0

    lax.fori_loop(core * half_groups, (core + 1) * half_groups, after_b, 0)
    back_b_pair.wait()
    lax.fori_loop((1 - core) * half_groups, (2 - core) * half_groups, after_b, 0)

    u, v = u_s[...], v_s[...]
    step = step_s[...]
    rate_gain = jnp.exp(rate)
    dlog = lane_sums(u - v, True)
    dstep = v / step - rate_gain * dlog
    draw = dstep / (1.0 + jnp.exp(-z))
    dt_out[...] = draw
    outs[2].start()
    rate_sum = jnp.sum(dlog * (-rate_gain * step), axis=1, keepdims=True)
    bias_sum = jnp.sum(draw, axis=1, keepdims=True)
    skip_sum = jnp.sum(sk_s[...], axis=1, keepdims=True)
    lanes = lax.broadcasted_iota(jnp.int32, square, 1)
    share[...] = jnp.where(lanes == 0, rate_sum, jnp.where(lanes == 1, bias_sum, jnp.where(lanes == 2, skip_sum, 0.0)))

    def eight(d):
        return pl.ds(pl.multiple_of(d * 8, 8), 8)

    share_got[dp] = share[eight(dp), :]
    to_all(lambda k: share.at[eight(lax.rem(dp + k, n_dp))], share_got.at[dp], share_ss, share_rs, "dp", n_dp, dp)

    def finish(g, _):
        rows, heads = rows_of(g), heads_of(g)
        g8 = gt[rows, :].astype(F32)
        dx_out[:, rows] = jnp.transpose(d_t[rows, :] + spread(skip_s[heads, :]) * g8).astype(BF16)
        l_hi, l_lo = split(later[rows, :])
        db_out[...] += mul(txn_hi[:, rows], l_hi) + mul(txn_hi[:, rows], l_lo) + mul(txn_lo[:, rows], l_hi)
        return 0

    lax.fori_loop(0, GROUPS, finish, 0)
    outs[3].start()
    outs[4].start()

    to(share_got.at[seven], share_got.at[seven], share_ss.at[0], share_rs.at[0], {"dp": dp}).wait()
    summed = share_got[0]
    for k in range(1, n_dp):
        summed = summed + share_got[k]
    total[...] = summed
    outs[5].start()
    to_all(lambda k: total, total_got.at[me], total_ss, total_rs, "ctx", n_ctx, me)
    all_pieces(pre_b, b2_ss, b2_rs).wait_send()
    b1_all.wait_send()
    for copy in outs:
        copy.wait()
    last31 = pl.ds(0, n_ctx - 1)
    to(total_got.at[last31], total_got.at[last31], total_ss.at[0], total_rs.at[0], {"ctx": me}).wait()


def write(*refs):
    sources, targets, buffers, lines, in_sem, out_sem = refs[:6], refs[6:14], refs[14:20], refs[20], refs[21], refs[22]
    loads = [pltpu.make_async_copy(src, dst, in_sem.at[k]) for k, (src, dst) in enumerate(zip(sources, buffers))]
    loads = loads[5:] + loads[:5]
    for copy in loads:
        copy.start()
    kept = [*buffers[:5], lines.at[0], lines.at[1], lines.at[2]]
    stores = [pltpu.make_async_copy(src, dst, out_sem.at[k]) for k, (src, dst) in enumerate(zip(kept, targets))]
    loads[0].wait()
    totals = buffers[5]
    summed = totals[0]
    for k in range(1, totals.shape[0]):
        summed = summed + totals[k]
    turned = jnp.transpose(jnp.concatenate([summed] * 16, axis=0))
    for k in range(3):
        lines[k] = turned[k : k + 1, 0:8]
        stores[5 + k].start()
    for k in range(5):
        loads[1 + k].wait()
        stores[k].start()
    for copy in stores:
        copy.wait()


def local(x, b, c, raw, rate, bias, skip, g):
    n_dp, n_ctx = lax.axis_size("dp"), lax.axis_size("ctx")
    vmem = pl.BlockSpec(memory_space=pltpu.VMEM)
    hbm = pl.BlockSpec(memory_space=pltpu.HBM)
    wide = (ROWS, 128)
    half = (HALF, 128)
    small = (HEADS, 128)
    piece = (CHIPS, PIECE, 128)
    longer = (CHIPS, PIECE + 8, 128)
    few = (HEADS // 2, 128)
    packed = (2 * TOKENS + HEADS // 2, 128)

    def buf(shape, dtype=F32):
        return pltpu.VMEM(shape, dtype)

    def sems(count):
        return pltpu.SemaphoreType.DMA((count,))

    landing = [
        buf((TOKENS, ROWS), BF16), buf((TOKENS, ROWS), BF16), buf((TOKENS, ENTRIES)), buf((TOKENS, ENTRIES)), buf(small),
        buf((n_ctx, 8, 128)),
    ]
    scratch = [
        *landing[:5],
        buf((TOKENS, ROWS), BF16), buf((TOKENS, ENTRIES), BF16), buf((TOKENS, ENTRIES), BF16), buf(small),
        buf((TOKENS, ROWS), BF16), *[pltpu.SMEM((8,), F32)] * 3,
        buf(wide, BF16), buf(wide, BF16), buf((TOKENS, TOKENS)), buf((n_dp, 8, 128)),
        *[buf(small)] * 5, buf((GROUPS, TOKENS, GROUP)), buf((GROUPS, TOKENS, GROUP)),
        *[buf((TOKENS, ROWS), BF16)] * 4, buf(small), buf(small),
        buf(packed), buf(half), buf(half), buf(packed), buf(half), buf(half), buf(few), buf(few),
        buf(small), buf(few), buf(wide), buf(wide), buf(half), buf(half),
        buf(longer), buf(piece), buf(longer), buf(piece),
        buf(piece), buf(piece), buf(half), buf(half), buf(half), buf(half), buf(wide), buf(wide),
        buf(wide), buf(wide), buf((TOKENS, TOKENS)), buf(small), buf(small), buf(small),
        buf(small), buf((n_dp, 8, 128)), buf((8, 128)),
        sems(8), sems(6), sems(1), sems(1), sems(3), sems(3), *[sems(1)] * 8, sems(2), sems(2), *[sems(1)] * 4,
    ]
    wide_out = jax.ShapeDtypeStruct((TOKENS, ROWS), BF16)
    square_out = jax.ShapeDtypeStruct((TOKENS, ENTRIES), F32)
    dt_shape = jax.ShapeDtypeStruct((HEADS, TOKENS), F32)
    shapes = [wide_out, wide_out, square_out, square_out, dt_shape]
    results = pl.pallas_call(
        layer,
        out_shape=[*shapes, jax.ShapeDtypeStruct((n_ctx, 8, 128), F32)],
        in_specs=[hbm] * 8,
        out_specs=[hbm] * 6,
        scratch_shapes=scratch,
        compiler_params=pltpu.CompilerParams(collective_id=0, has_side_effects=True, vmem_limit_bytes=60 << 20),
        name="layer",
    )(x[0], b[0], c[0], raw[0], rate, bias, skip, g[0])
    y, dx, db, dc, dt, dr, dbias, dskip = pl.pallas_call(
        write,
        out_shape=[*shapes, *[jax.ShapeDtypeStruct((1, 8), F32)] * 3],
        in_specs=[hbm] * 6,
        out_specs=[hbm] * 8,
        scratch_shapes=[*landing, buf((3, 1, 8)), sems(6), sems(8)],
        compiler_params=pltpu.CompilerParams(vmem_limit_bytes=60 << 20),
        name="write",
    )(*results)
    return y[None], dx[None], db[None], dc[None], dt[None], dr.reshape(8), dbias.reshape(8), dskip.reshape(8)


def solution(mesh):
    tokens = P("dp", "ctx", None)
    strides = P("dp", None, "ctx")
    owned = P("dp")
    return jax.shard_map(
        local,
        mesh=mesh,
        in_specs=(tokens, tokens, tokens, strides, owned, owned, owned, tokens),
        out_specs=(tokens, tokens, tokens, tokens, strides, owned, owned, owned),
        check_vma=False,
    )
```

```python
import jax
import jax.numpy as jnp
from jax import lax
from jax.experimental import pallas as pl
from jax.experimental.pallas import tpu as pltpu
from jax.sharding import PartitionSpec as P

MESH = pl.DeviceIdType.MESH
F32, BF16 = jnp.float32, jnp.bfloat16

TOKENS = 128
HEADS = 64
WIDTH = 32
ENTRIES = 128
ROWS = HEADS * WIDTH
HALF = ROWS // 2
GROUP = 8
GROUP_ROWS = GROUP * WIDTH
GROUPS = HEADS // GROUP
CHIPS = 16
PIECE = HALF // CHIPS


def split(value):
    high = value.astype(BF16)
    return high, (value - high.astype(F32)).astype(BF16)


def mul(a, b):
    return jnp.dot(a, b, preferred_element_type=F32)


def mul_nt(a, b):
    return lax.dot_general(a, b, (((1,), (1,)), ((), ())), preferred_element_type=F32)


def spread(rows, width=WIDTH):
    count = rows.shape[0]
    parts = [jnp.broadcast_to(rows[k : k + 1, :], (width, rows.shape[1])) for k in range(count)]
    return jnp.concatenate(parts, axis=0)


def folded(value, count):
    return jnp.sum(value.reshape(count, WIDTH, value.shape[1]), axis=1)


def lane_sums(value, reverse):
    lanes = lax.broadcasted_iota(jnp.int32, value.shape, 1)
    size = value.shape[1]
    shift = 1
    while shift < size:
        if reverse:
            moved = jnp.where(lanes < size - shift, pltpu.roll(value, size - shift, 1), 0.0)
        else:
            moved = jnp.where(lanes >= shift, pltpu.roll(value, shift, 1), 0.0)
        value = value + moved
        shift *= 2
    return value
SPLIT = (1, 3, 5)
FAR = 1


def layer(
    x_hbm, b_hbm, c_hbm, raw_hbm, rate_hbm, bias_hbm, skip_hbm, g_hbm,
    y_hbm, dx_hbm, db_hbm, dc_hbm, dt_hbm, total_got,
    y_out, dx_out, db_out, dc_out, dt_out,
    x_ref, b_ref, c_ref, raw_ref, g_ref, rate_ref, bias_ref, skip_ref,
    xt, gt, gram_t, par_recv, cum_s, step_s, tail_s, grow_s, skip_s, cum_col, step_col,
    txn_hi, txn_lo, egn_hi, egn_lo, rate_s, bias_s, pack_own, x_own, g_own, pack_other, x_other, g_other, tail_o, grow_o,
    ends_own, ends_other, state, grad, state_other, grad_other,
    tot_f, tot_b, got_f, got_b, pre_f, pre_b, in_f, in_b, back_f, back_b, carried, later,
    y_t, d_t, dgram_t, u_s, v_s, sk_s, z_s, z_o, step_o, u_o, v_o, sk_o, vi_s, intra_own, intra_other, dt_sent, share, share_got, total,
    in_sem, out_sem, par_ss, par_rs, mid_ss, mid_rs, pair_ss, pair_rs, f1_ss, f1_rs, b1_ss, b1_rs, f2_ss, f2_rs, b2_ss, b2_rs,
    back_ss, back_rs, share_ss, share_rs, total_ss, total_rs,
):
    me = lax.axis_index("ctx")
    dp = lax.axis_index("dp")
    n_dp = lax.axis_size("dp")
    n_ctx = lax.axis_size("ctx")
    core = lax.rem(me, 2)
    chip = me // 2
    partner = chip * 2 + 1 - core
    first = core == 0

    def to(src, dst, ss, rs, where):
        return pltpu.make_async_remote_copy(src, dst, ss, rs, device_id=where, device_id_type=MESH)

    barrier = pltpu.get_barrier_semaphore()
    for k in range(1, n_dp):
        pl.semaphore_signal(barrier, 1, device_id={"dp": lax.rem(dp + k, n_dp)}, device_id_type=MESH)
    for k in range(1, n_ctx):
        pl.semaphore_signal(barrier, 1, device_id={"ctx": lax.rem(me + k, n_ctx)}, device_id_type=MESH)

    loads = [
        pltpu.make_async_copy(src, dst, in_sem.at[k])
        for k, (src, dst) in enumerate(
            (
                (rate_hbm, rate_ref), (bias_hbm, bias_ref), (skip_hbm, skip_ref), (raw_hbm, raw_ref),
                (x_hbm, x_ref), (b_hbm, b_ref), (g_hbm, g_ref), (c_hbm, c_ref),
            )
        )
    ]
    for copy in loads:
        copy.start()
    for copy in loads[:3]:
        copy.wait()

    lanes8 = lax.broadcasted_iota(jnp.int32, (8, 128), 1)
    rows8 = lax.broadcasted_iota(jnp.int32, (8, 128), 0)
    tile = jnp.zeros((8, 128), F32)
    for row, ref in enumerate((rate_ref, bias_ref, skip_ref)):
        for j in range(8):
            here = jnp.logical_and(rows8 == row, lanes8 == dp * 8 + j)
            tile = jnp.where(here, ref[j], tile)
    par_recv[dp] = tile

    pl.semaphore_wait(barrier, n_dp + n_ctx - 2)

    def to_all(src, dst, ss, rs, axis, size, index):
        for k in range(1, size):
            to(src(k), dst, ss.at[0], rs.at[0], {axis: lax.rem(index + k, size)}).start()

    to_all(lambda k: par_recv.at[dp], par_recv.at[dp], par_ss, par_rs, "dp", n_dp, dp)

    there = {"ctx": partner}
    pack_pair = to(pack_own, pack_other, pair_ss.at[0], pair_rs.at[0], there)
    x_pair = to(x_own, x_other, pair_ss.at[1], pair_rs.at[1], there)
    g_pair = to(g_own, g_other, pair_ss.at[2], pair_rs.at[2], there)
    half_groups = GROUPS // 2
    heads_here = HEADS // 2
    for copy in loads[3:]:
        copy.wait()
    pack_own[0:TOKENS, :] = b_ref[...].astype(F32)
    pack_own[TOKENS : 2 * TOKENS, :] = c_ref[...].astype(F32)
    pack_own[2 * TOKENS :, :] = raw_ref[pl.ds(pl.multiple_of((1 - core) * heads_here, heads_here), heads_here), :]
    pack_pair.start()

    def turned(src, dst, sent, half):
        for k in range(half_groups):
            rows = pl.ds(pl.multiple_of(half * HALF + k * GROUP_ROWS, GROUP_ROWS), GROUP_ROWS)
            value = jnp.transpose(src[:, rows].astype(F32))
            dst[rows, :] = value.astype(BF16)
            if sent is not None:
                sent[k * GROUP_ROWS : (k + 1) * GROUP_ROWS, :] = value

    turned(x_ref, xt, x_own, 1 - core)
    x_pair.start()
    turned(g_ref, gt, g_own, 1 - core)
    g_pair.start()
    turned(x_ref, xt, None, core)
    turned(g_ref, gt, None, core)
    gram_t[...] = mul_nt(b_ref[...], c_ref[...])

    seven = pl.ds(0, n_dp - 1)
    to(par_recv.at[seven], par_recv.at[seven], par_ss.at[0], par_rs.at[0], {"dp": dp}).wait()

    params = par_recv[0]
    for k in range(1, n_dp):
        params = params + par_recv[k]
    columns = jnp.transpose(jnp.concatenate([params] * 16, axis=0))[:HEADS, :]
    square = (HEADS, 128)
    rate = jnp.broadcast_to(columns[:, 0:1], square)
    bias = jnp.broadcast_to(columns[:, 1:2], square)
    skip_s[...] = jnp.broadcast_to(columns[:, 2:3], square)
    rate_s[...] = rate
    bias_s[...] = bias

    def steps_of(raw, rate, bias):
        z = raw + bias
        step = jnp.maximum(z, 0.0) + jnp.log1p(jnp.exp(-jnp.abs(z)))
        cum = lane_sums(-jnp.exp(rate) * step, False)
        return z, step, cum, jnp.broadcast_to(cum[:, 127:128], cum.shape)

    z, step, cum, last = steps_of(raw_ref[...], rate, bias)
    cum_s[...] = cum
    step_s[...] = step
    tail_s[...] = jnp.exp(last - cum) * step
    grow_s[...] = jnp.exp(cum)
    ends_own[...] = jnp.exp(last)
    here = pl.ds(pl.multiple_of(core * heads_here, heads_here), heads_here)
    pack_pair.wait()
    z_s[...] = z
    z_other, step_other, cum_o, last_o = steps_of(pack_other[2 * TOKENS :, :], rate_s[here, :], bias_s[here, :])
    z_o[...] = z_other
    step_o[...] = step_other
    tail_o[...] = jnp.exp(last_o - cum_o) * step_other
    grow_o[...] = jnp.exp(cum_o)
    ends_other[...] = jnp.exp(last_o)
    b_other = pack_other[0:TOKENS, :].astype(BF16)
    c_other = pack_other[TOKENS : 2 * TOKENS, :].astype(BF16)

    def rows_of(g):
        return pl.ds(pl.multiple_of(g * GROUP_ROWS, GROUP_ROWS), GROUP_ROWS)

    def heads_of(g):
        return pl.ds(pl.multiple_of(g * GROUP, GROUP), GROUP)

    outs = [
        pltpu.make_async_copy(src, dst, out_sem.at[k])
        for k, (src, dst) in enumerate(
            (
                (y_out, y_hbm), (dc_out, dc_hbm), (dt_out, dt_hbm), (dx_out, dx_hbm), (db_out, db_hbm),
                (total, total_got.at[chip]),
            )
        )
    ]

    mine = pl.ds(pl.multiple_of(core * HALF, HALF), HALF)
    base = core * (HEADS // 2)

    def row_of(ref, head):
        return jnp.broadcast_to(ref[pl.ds(head, 1), :], (WIDTH, 128))

    def two(ref, r):
        at = base + 2 * r if ref is ends_own else 2 * r
        return jnp.concatenate([row_of(ref, at), row_of(ref, at + 1)], axis=0)

    def piece_rows(r):
        return pl.ds(pl.multiple_of(core * HALF + r * PIECE, PIECE), PIECE)

    def chip_of(k):
        return lax.rem(chip + k, CHIPS)

    def chip_id(k):
        return {"ctx": chip_of(k) * 2 + core}

    spot = pl.ds(pl.multiple_of(chip * PIECE, PIECE), PIECE)
    others = pl.ds(0, CHIPS - 1)
    most = pl.ds(0, HALF - PIECE)

    def out_pieces(src, dst, ss, rs):
        for k in range(1, CHIPS):
            to(src.at[chip_of(k)], dst, ss.at[0], rs.at[0], chip_id(k)).start()

    def all_pieces(src, ss, rs):
        return to(src.at[others], src.at[others], ss.at[0], rs.at[0], there)

    def product(rows, gains, entries):
        hi, lo = split(rows.astype(F32) * spread(gains))
        return mul(hi, entries) + mul(lo, entries)

    row = chip // 4

    def send(src, dst, ss, rs, g):
        for j in range(4):
            target = g * 4 + lax.rem(chip + j, 4)

            @pl.when(target != chip)
            def _():
                to(src.at[target], dst, ss.at[0], rs.at[0], {"ctx": target * 2 + core}).start()

    def totals_f(k, _):
        g = lax.rem(row + k + 1, 4)
        rows, heads = rows_of(core * half_groups + g), heads_of(core * half_groups + g)
        local_rows, local_heads = rows_of(g), heads_of(g)
        own = product(xt[rows, :], tail_s[heads, :], b_ref[...])
        other = product(x_other[local_rows, :], tail_o[local_heads, :], b_other)
        state[rows, :] = own
        state_other[local_rows, :] = other
        e_own, e_other = ends_own[heads, :], ends_other[local_heads, :]
        both = jnp.where(first, spread(e_other) * own + other, own + spread(e_own) * other)
        decay = e_own * e_other
        for j in range(4):
            tot_f[g * 4 + j, 0:PIECE, :] = both[j * PIECE : (j + 1) * PIECE, :]
            tot_f[g * 4 + j, PIECE : PIECE + 8, :] = jnp.concatenate([decay[2 * j : 2 * j + 2, :]] * 4, axis=0)
        send(tot_f, got_f.at[chip], f1_ss, f1_rs, g)
        return 0

    def totals_b(k, _):
        g = lax.rem(row + k + 1, 4)
        rows, heads = rows_of(core * half_groups + g), heads_of(core * half_groups + g)
        local_rows, local_heads = rows_of(g), heads_of(g)
        own = product(gt[rows, :], grow_s[heads, :], c_ref[...])
        other = product(g_other[local_rows, :], grow_o[local_heads, :], c_other)
        grad[rows, :] = own
        grad_other[local_rows, :] = other
        e_own, e_other = ends_own[heads, :], ends_other[local_heads, :]
        both = jnp.where(first, own + spread(e_own) * other, spread(e_other) * own + other)
        for j in range(4):
            tot_b[g * 4 + j] = both[j * PIECE : (j + 1) * PIECE, :]
        return 0

    x_pair.wait()
    lax.fori_loop(0, half_groups, totals_f, 0)
    got_f[chip] = tot_f[chip]
    g_pair.wait()
    lax.fori_loop(0, half_groups, totals_b, 0)
    got_b[chip] = tot_b[chip]

    def padded(value):
        return jnp.transpose(jnp.concatenate([value, value], axis=0))

    cum_t, step_t = padded(cum_s[...]), padded(step_s[...])
    for k in range(GROUPS):
        cum_col[k] = cum_t[:, k * GROUP : (k + 1) * GROUP]
        step_col[k] = step_t[:, k * GROUP : (k + 1) * GROUP]
    dgram_t[...] = jnp.zeros_like(dgram_t)

    def within(g, _):
        rows, heads = rows_of(g), heads_of(g)
        cum8, cumc, stepc = cum_s[heads, :], cum_col[g], step_col[g]
        xt8, gt8 = xt[rows, :], gt[rows, :]
        above = lax.broadcasted_iota(jnp.int32, (TOKENS, TOKENS), 0) <= lax.broadcasted_iota(
            jnp.int32, (TOKENS, TOKENS), 1
        )
        gram = gram_t[...]
        acc = dgram_t[...]
        none = jnp.zeros((WIDTH, TOKENS), BF16)
        for quad in range(2):
            xq = x_ref[:, pl.ds(pl.multiple_of(g * GROUP_ROWS + quad * 128, 128), 128)]
            for j in range(4):
                k = quad * 4 + j
                at = slice(k * WIDTH, (k + 1) * WIDTH)
                g_rows = gt8[at, :]
                weights_g = jnp.concatenate([g_rows if i == j else none for i in range(4)], axis=0)
                dw = mul(xq, weights_g)
                diff = jnp.broadcast_to(cum8[k : k + 1, :], (TOKENS, TOKENS)) - jnp.broadcast_to(
                    cumc[:, k : k + 1], (TOKENS, TOKENS)
                )
                seg = jnp.exp(jnp.where(above, diff, -1e30))
                factor = seg * jnp.broadcast_to(stepc[:, k : k + 1], (TOKENS, TOKENS))
                acc = acc + dw * factor
                hi, lo = split(gram * factor)
                inner = mul(xt8[at, :], hi) + mul(xt8[at, :], lo)
                back = mul_nt(g_rows, hi) + mul_nt(g_rows, lo)
                out = pl.ds(pl.multiple_of(g * GROUP_ROWS + k * WIDTH, WIDTH), WIDTH)
                y_t[out, :] = inner
                d_t[out, :] = back
        dgram_t[...] = acc
        x8, g8 = xt8.astype(F32), gt8.astype(F32)
        sk_s[heads, :] = folded(x8 * g8, GROUP)
        u_s[heads, :] = folded(g8 * y_t[rows, :], GROUP)
        vi_s[heads, :] = folded(x8 * d_t[rows, :], GROUP)
        return 0

    def turn_of(src, gains, hi_out, lo_out):
        def turn(g, _):
            rows, heads = rows_of(g), heads_of(g)
            hi, lo = split(jnp.transpose(src[rows, :].astype(F32) * spread(gains[heads, :])))
            hi_out[:, rows] = hi
            lo_out[:, rows] = lo
            return 0

        lax.fori_loop(0, GROUPS, turn, 0)

    lax.fori_loop(0, SPLIT[0], within, 0)
    f1_all = all_pieces(tot_f, f1_ss, f1_rs)
    f1_all.wait_send()
    out_pieces(tot_b, got_b.at[chip], b1_ss, b1_rs)

    lax.fori_loop(SPLIT[0], SPLIT[1], within, 0)

    def decay_of(q):
        return jnp.concatenate(
            [jnp.broadcast_to(got_f[q, PIECE + k : PIECE + k + 1, :], (WIDTH, 128)) for k in range(2)], axis=0
        )

    f1_all.wait_recv()
    run = jnp.zeros((PIECE, 128), F32)
    for q in range(CHIPS):
        pre_f[q] = run
        run = decay_of(q) * run + got_f[q, 0:PIECE, :]
    in_f[spot, :] = pre_f[chip]
    b1_all = all_pieces(tot_b, b1_ss, b1_rs)
    out_pieces(pre_f, in_f.at[spot], f2_ss, f2_rs)

    lax.fori_loop(SPLIT[1], SPLIT[2], within, 0)

    b1_all.wait_recv()
    run = jnp.zeros((PIECE, 128), F32)
    for q in reversed(range(CHIPS)):
        pre_b[q] = run
        run = decay_of(q) * run + got_b[q]
    in_b[spot, :] = pre_b[chip]
    all_pieces(pre_f, f2_ss, f2_rs).wait_send()
    out_pieces(pre_b, in_b.at[spot], b2_ss, b2_rs)

    lax.fori_loop(SPLIT[2], GROUPS, within, 0)

    far = pl.ds(pl.multiple_of((1 - core) * heads_here, heads_here), heads_here)
    intra_own[0:heads_here, :] = u_s[far, :]
    intra_own[heads_here:, :] = vi_s[far, :]
    intra_pair = to(intra_own, intra_other, mid_ss.at[0], mid_rs.at[0], there)
    intra_pair.start()
    turn_of(gt, grow_s, egn_hi, egn_lo)
    turn_of(xt, tail_s, txn_hi, txn_lo)
    g_hi, g_lo = split(dgram_t[...])
    db_out[...] = mul(g_hi, c_ref[...]) + mul(g_lo, c_ref[...])
    t_hi, t_lo = split(jnp.transpose(dgram_t[...]))
    dc_out[...] = mul(t_hi, b_ref[...]) + mul(t_lo, b_ref[...])

    back_f_pair = to(back_f, carried.at[mine], back_ss.at[0], back_rs.at[0], there)
    back_b_pair = to(back_b, later.at[mine], back_ss.at[1], back_rs.at[1], there)
    to(in_f.at[most], in_f.at[most], f2_ss.at[0], f2_rs.at[0], there).wait_recv()
    for r in range(CHIPS):
        at = slice(r * PIECE, (r + 1) * PIECE)
        e_own, e_other = two(ends_own, r), two(ends_other, r)
        chips = in_f[at, :]
        carried[piece_rows(r), :] = jnp.where(first, chips, e_other * chips + state_other[at, :])
        back_f[at, :] = jnp.where(first, e_own * chips + state[piece_rows(r), :], chips)
    back_f_pair.start()
    def read(rows, heads):
        a_hi, a_lo = split(carried[rows, :])
        return spread(grow_s[heads, :]) * (mul_nt(a_hi, c_ref[...]) + mul_nt(a_lo, c_ref[...]))

    def own_f(k, _):
        g = core * half_groups + k
        rows, heads = rows_of(g), heads_of(g)
        part = read(rows, heads)
        y_t[rows, :] += part
        u_s[heads, :] += folded(gt[rows, :].astype(F32) * part, GROUP)
        return 0

    lax.fori_loop(0, half_groups, own_f, 0)
    intra_pair.wait()

    def other_f(g, _):
        rows, heads = rows_of(g), heads_of(g)
        a_hi, a_lo = split(back_f[rows, :])
        readout = mul_nt(a_hi, c_other) + mul_nt(a_lo, c_other)
        g8 = g_other[rows, :]
        u_o[heads, :] = intra_other[heads, :] + grow_o[heads, :] * folded(g8 * readout, GROUP)
        sk_o[heads, :] = folded(x_other[rows, :] * g8, GROUP)
        return 0

    lax.fori_loop(0, half_groups, other_f, 0)

    to(in_b.at[most], in_b.at[most], b2_ss.at[0], b2_rs.at[0], there).wait_recv()
    for r in range(CHIPS):
        at = slice(r * PIECE, (r + 1) * PIECE)
        e_own, e_other = two(ends_own, r), two(ends_other, r)
        chips = in_b[at, :]
        later[piece_rows(r), :] = jnp.where(first, e_other * chips + grad_other[at, :], chips)
        back_b[at, :] = jnp.where(first, chips, e_own * chips + grad[piece_rows(r), :])
    back_b_pair.start()

    lanes8 = lax.broadcasted_iota(jnp.int32, (GROUP, 128), 1)

    def at_end(value):
        value = jnp.broadcast_to(jnp.sum(value, axis=1, keepdims=True), (GROUP, 128))
        return jnp.where(lanes8 == 127, value, 0.0)

    def from_later(l, gains, entries):
        l_hi, l_lo = split(l)
        return spread(gains) * (mul_nt(l_hi, entries) + mul_nt(l_lo, entries))

    def after_b(k, _):
        g = core * half_groups + k
        rows, heads = rows_of(g), heads_of(g)
        l = later[rows, :]
        tq = from_later(l, tail_s[heads, :], b_ref[...])
        d_t[rows, :] += tq
        from_tail = folded(xt[rows, :].astype(F32) * tq, GROUP)
        v_s[heads, :] = vi_s[heads, :] + from_tail
        u_s[heads, :] += at_end(from_tail + ends_own[heads, :] * folded(carried[rows, :] * l, GROUP))
        rows, heads = rows_of(k), heads_of(k)
        l = back_b[rows, :]
        from_tail = folded(x_other[rows, :] * from_later(l, tail_o[heads, :], b_other), GROUP)
        v_o[heads, :] = intra_other[pl.ds(pl.multiple_of(heads_here + k * GROUP, GROUP), GROUP), :] + from_tail
        u_o[heads, :] += at_end(from_tail + ends_other[heads, :] * folded(back_f[rows, :] * l, GROUP))
        return 0

    lax.fori_loop(0, half_groups, after_b, 0)

    def pair_of(own, other):
        return jnp.concatenate([own[here, :], other[...]], axis=0)

    u, v, step, zs = pair_of(u_s, u_o), pair_of(v_s, v_o), pair_of(step_s, step_o), pair_of(z_s, z_o)
    rate_gain = jnp.exp(pair_of(rate_s, rate_s.at[here]))
    dlog = lane_sums(u - v, True)
    dstep = v / step - rate_gain * dlog
    draw = dstep / (1.0 + jnp.exp(-zs))
    rate_sum = jnp.sum(dlog * (-rate_gain * step), axis=1, keepdims=True)
    bias_sum = jnp.sum(draw, axis=1, keepdims=True)
    skip_sum = jnp.sum(pair_of(sk_s, sk_o), axis=1, keepdims=True)
    lanes = lax.broadcasted_iota(jnp.int32, square, 1)
    sums = jnp.where(lanes == 0, rate_sum, jnp.where(lanes == 1, bias_sum, jnp.where(lanes == 2, skip_sum, 0.0)))
    share[...] = sums[0:heads_here, :] + sums[heads_here:, :]

    owners = n_dp // 2
    owner = dp // owners == core
    for k in range(owners):
        plane = core * owners + k

        @pl.when(plane != dp)
        def _():
            to(share.at[k * 8 : k * 8 + 8], share_got.at[dp], share_ss.at[0], share_rs.at[0], {"dp": plane}).start()

        @pl.when(plane == dp)
        def _():
            share_got[dp] = share[k * 8 : k * 8 + 8, :]

    dt_out[here, :] = draw[0:heads_here, :]
    dt_sent[...] = draw[heads_here:, :]
    dt_pair = to(dt_sent, dt_out.at[here], mid_ss.at[1], mid_rs.at[1], there)
    dt_pair.start()

    def finish(g, _):
        rows, heads = rows_of(g), heads_of(g)
        gains = spread(skip_s[heads, :])
        y_out[:, rows] = jnp.transpose(y_t[rows, :] + gains * xt[rows, :].astype(F32)).astype(BF16)
        dx_out[:, rows] = jnp.transpose(d_t[rows, :] + gains * gt[rows, :].astype(F32)).astype(BF16)
        a_hi, a_lo = split(carried[rows, :])
        l_hi, l_lo = split(later[rows, :])
        dc_out[...] += mul(egn_hi[:, rows], a_hi) + mul(egn_hi[:, rows], a_lo) + mul(egn_lo[:, rows], a_hi)
        db_out[...] += mul(txn_hi[:, rows], l_hi) + mul(txn_hi[:, rows], l_lo) + mul(txn_lo[:, rows], l_hi)
        return 0

    def finish_far(k, _):
        g = (1 - core) * half_groups + k
        rows, heads = rows_of(g), heads_of(g)
        y_t[rows, :] += read(rows, heads)
        d_t[rows, :] += from_later(later[rows, :], tail_s[heads, :], b_ref[...])
        return finish(g, 0)

    def total_sums():
        @pl.when(owner)
        def _():
            to(share_got.at[seven], share_got.at[seven], share_ss.at[0], share_rs.at[0], {"dp": dp}).wait_recv()
            summed = share_got[0]
            for k in range(1, n_dp):
                summed = summed + share_got[k]
            total[...] = summed
            outs[5].start()
            to_all(lambda k: total, total_got.at[chip], total_ss, total_rs, "ctx", n_ctx, me)

    lax.fori_loop(core * half_groups, (core + 1) * half_groups, finish, 0)
    back_f_pair.wait()
    back_b_pair.wait()
    lax.fori_loop(0, FAR, finish_far, 0)
    total_sums()
    lax.fori_loop(FAR, half_groups, finish_far, 0)
    for k in (0, 1, 3, 4):
        outs[k].start()
    dt_pair.wait()
    outs[2].start()
    b1_all.wait_send()
    all_pieces(pre_b, b2_ss, b2_rs).wait_send()
    for copy in outs[:5]:
        copy.wait()

    def tiles(ref, count):
        return ref.at[pl.ds(0, count)]

    def shares_sent(count):
        part = share.at[0 : count * 8]
        to(part, part, share_ss.at[0], share_rs.at[0], there).wait_send()

    def totals_got(count):
        part = tiles(total_got, count)
        to(part, part, total_ss.at[0], total_rs.at[0], there).wait_recv()

    @pl.when(owner)
    def _():
        shares_sent(owners - 1)
        outs[5].wait()
        part = state.at[0 : (n_ctx - 1) * 8]
        to(part, part, total_ss.at[0], total_rs.at[0], there).wait_send()
        totals_got(CHIPS - 1)

    @pl.when(jnp.logical_not(owner))
    def _():
        shares_sent(owners)
        totals_got(CHIPS)


def write(*refs):
    sources, targets, buffers, lines, in_sem, out_sem = refs[:6], refs[6:14], refs[14:20], refs[20], refs[21], refs[22]
    loads = [pltpu.make_async_copy(src, dst, in_sem.at[k]) for k, (src, dst) in enumerate(zip(sources, buffers))]
    loads = loads[5:] + loads[:5]
    for copy in loads:
        copy.start()
    kept = [*buffers[:5], lines.at[0], lines.at[1], lines.at[2]]
    stores = [pltpu.make_async_copy(src, dst, out_sem.at[k]) for k, (src, dst) in enumerate(zip(kept, targets))]
    loads[0].wait()
    totals = buffers[5]
    summed = totals[0]
    for k in range(1, totals.shape[0]):
        summed = summed + totals[k]
    turned = jnp.transpose(jnp.concatenate([summed] * 16, axis=0))
    for k in range(3):
        lines[k] = turned[k : k + 1, 0:8]
        stores[5 + k].start()
    for k in range(5):
        loads[1 + k].wait()
        stores[k].start()
    for copy in stores:
        copy.wait()


def local(x, b, c, raw, rate, bias, skip, g):
    n_dp = lax.axis_size("dp")
    vmem = pl.BlockSpec(memory_space=pltpu.VMEM)
    hbm = pl.BlockSpec(memory_space=pltpu.HBM)
    wide = (ROWS, 128)
    half = (HALF, 128)
    small = (HEADS, 128)
    piece = (CHIPS, PIECE, 128)
    longer = (CHIPS, PIECE + 8, 128)
    few = (HEADS // 2, 128)
    packed = (2 * TOKENS + HEADS // 2, 128)

    def buf(shape, dtype=F32):
        return pltpu.VMEM(shape, dtype)

    def sems(count):
        return pltpu.SemaphoreType.DMA((count,))

    landing = [
        buf((TOKENS, ROWS), BF16), buf((TOKENS, ROWS), BF16), buf((TOKENS, ENTRIES)), buf((TOKENS, ENTRIES)), buf(small),
        buf((CHIPS, 8, 128)),
    ]
    scratch = [
        *landing[:5],
        buf((TOKENS, ROWS), BF16), buf((TOKENS, ENTRIES), BF16), buf((TOKENS, ENTRIES), BF16), buf(small),
        buf((TOKENS, ROWS), BF16), *[pltpu.SMEM((8,), F32)] * 3,
        buf(wide, BF16), buf(wide, BF16), buf((TOKENS, TOKENS)), buf((n_dp, 8, 128)),
        *[buf(small)] * 5, buf((GROUPS, TOKENS, GROUP)), buf((GROUPS, TOKENS, GROUP)),
        *[buf((TOKENS, ROWS), BF16)] * 4, buf(small), buf(small),
        buf(packed), buf(half), buf(half), buf(packed), buf(half), buf(half), buf(few), buf(few),
        buf(small), buf(few), buf(wide), buf(wide), buf(half), buf(half),
        buf(longer), buf(piece), buf(longer), buf(piece),
        buf(piece), buf(piece), buf(half), buf(half), buf(half), buf(half), buf(wide), buf(wide),
        buf(wide), buf(wide), buf((TOKENS, TOKENS)), *[buf(small)] * 4, *[buf(few)] * 5, *[buf(small)] * 3, buf(few),
        buf(few), buf((n_dp, 8, 128)), buf((8, 128)),
        sems(8), sems(6), sems(1), sems(1), sems(2), sems(2), sems(3), sems(3), *[sems(1)] * 8, sems(2), sems(2), *[sems(1)] * 4,
    ]
    wide_out = jax.ShapeDtypeStruct((TOKENS, ROWS), BF16)
    square_out = jax.ShapeDtypeStruct((TOKENS, ENTRIES), F32)
    dt_shape = jax.ShapeDtypeStruct((HEADS, TOKENS), F32)
    shapes = [wide_out, wide_out, square_out, square_out, dt_shape]
    results = pl.pallas_call(
        layer,
        out_shape=[*shapes, jax.ShapeDtypeStruct((CHIPS, 8, 128), F32)],
        in_specs=[hbm] * 8,
        out_specs=[hbm] * 6,
        scratch_shapes=scratch,
        compiler_params=pltpu.CompilerParams(collective_id=0, has_side_effects=True, vmem_limit_bytes=60 << 20),
        name="layer",
    )(x[0], b[0], c[0], raw[0], rate, bias, skip, g[0])
    y, dx, db, dc, dt, dr, dbias, dskip = pl.pallas_call(
        write,
        out_shape=[*shapes, *[jax.ShapeDtypeStruct((1, 8), F32)] * 3],
        in_specs=[hbm] * 6,
        out_specs=[hbm] * 8,
        scratch_shapes=[*landing, buf((3, 1, 8)), sems(6), sems(8)],
        compiler_params=pltpu.CompilerParams(vmem_limit_bytes=60 << 20),
        name="write",
    )(*results)
    return y[None], dx[None], db[None], dc[None], dt[None], dr.reshape(8), dbias.reshape(8), dskip.reshape(8)


def solution(mesh):
    tokens = P("dp", "ctx", None)
    strides = P("dp", None, "ctx")
    owned = P("dp")
    return jax.shard_map(
        local,
        mesh=mesh,
        in_specs=(tokens, tokens, tokens, strides, owned, owned, owned, tokens),
        out_specs=(tokens, tokens, tokens, tokens, strides, owned, owned, owned),
        check_vma=False,
    )
```

```python
import jax
import jax.numpy as jnp
from jax import lax
from jax.experimental import pallas as pl
from jax.experimental.pallas import tpu as pltpu
from jax.sharding import PartitionSpec as P

MESH = pl.DeviceIdType.MESH
F32, BF16 = jnp.float32, jnp.bfloat16

TOKENS = 128
HEADS = 64
WIDTH = 32
ENTRIES = 128
ROWS = HEADS * WIDTH
HALF = ROWS // 2
GROUP = 8
GROUP_ROWS = GROUP * WIDTH
GROUPS = HEADS // GROUP
CHIPS = 16
PIECE = HALF // CHIPS


def split(value):
    high = value.astype(BF16)
    return high, (value - high.astype(F32)).astype(BF16)


def mul(a, b):
    return jnp.dot(a, b, preferred_element_type=F32)


def mul_nt(a, b):
    return lax.dot_general(a, b, (((1,), (1,)), ((), ())), preferred_element_type=F32)


def spread(rows, width=WIDTH):
    count = rows.shape[0]
    parts = [jnp.broadcast_to(rows[k : k + 1, :], (width, rows.shape[1])) for k in range(count)]
    return jnp.concatenate(parts, axis=0)


def folded(value, count):
    return jnp.sum(value.reshape(count, WIDTH, value.shape[1]), axis=1)


def lane_sums(value, reverse):
    lanes = lax.broadcasted_iota(jnp.int32, value.shape, 1)
    size = value.shape[1]
    shift = 1
    while shift < size:
        if reverse:
            moved = jnp.where(lanes < size - shift, pltpu.roll(value, size - shift, 1), 0.0)
        else:
            moved = jnp.where(lanes >= shift, pltpu.roll(value, shift, 1), 0.0)
        value = value + moved
        shift *= 2
    return value
SPLIT = (0, 3, 5)
FAR = 1


def far_first(size):
    return sorted(range(1, size), key=lambda k: -min(k, size - k))


def layer(
    x_hbm, b_hbm, c_hbm, raw_hbm, rate_hbm, bias_hbm, skip_hbm, g_hbm,
    y_hbm, dx_hbm, db_hbm, dc_hbm, dt_hbm, total_got,
    y_out, dx_out, db_out, dc_out, dt_out,
    x_ref, b_ref, c_ref, raw_ref, g_ref, rate_ref, bias_ref, skip_ref,
    xt, gt, gram_t, par_recv, cum_s, step_s, tail_s, grow_s, skip_s, cum_col, step_col,
    txn_hi, txn_lo, egn_hi, egn_lo, rate_s, bias_s, pack_own, x_own, g_own, pack_other, x_other, g_other, tail_o, grow_o,
    ends_own, ends_other, state, grad, state_other, grad_other,
    tot_f, tot_b, got_f, got_b, pre_f, pre_b, in_f, in_b, back_f, back_b, carried, later,
    y_t, d_t, dgram_t, u_s, v_s, sk_s, z_s, z_o, step_o, u_o, v_o, sk_o, vi_s, intra_own, intra_other, dt_sent, share, share_got, total,
    in_sem, out_sem, par_ss, par_rs, mid_ss, mid_rs, pair_ss, pair_rs, f1_ss, f1_rs, b1_ss, b1_rs, f2_ss, f2_rs, b2_ss, b2_rs,
    back_ss, back_rs, share_ss, share_rs, total_ss, total_rs,
):
    me = lax.axis_index("ctx")
    dp = lax.axis_index("dp")
    n_dp = lax.axis_size("dp")
    n_ctx = lax.axis_size("ctx")
    core = lax.rem(me, 2)
    chip = me // 2
    partner = chip * 2 + 1 - core
    first = core == 0

    def to(src, dst, ss, rs, where):
        return pltpu.make_async_remote_copy(src, dst, ss, rs, device_id=where, device_id_type=MESH)

    loads = [
        pltpu.make_async_copy(src, dst, in_sem.at[k])
        for k, (src, dst) in enumerate(
            (
                (rate_hbm, rate_ref), (bias_hbm, bias_ref), (skip_hbm, skip_ref), (raw_hbm, raw_ref),
                (x_hbm, x_ref), (b_hbm, b_ref), (g_hbm, g_ref), (c_hbm, c_ref),
            )
        )
    ]
    for copy in loads:
        copy.start()
    barrier = pltpu.get_barrier_semaphore()
    for k in far_first(n_dp):
        pl.semaphore_signal(barrier, 1, device_id={"dp": lax.rem(dp + k, n_dp)}, device_id_type=MESH)
    for k in far_first(n_ctx):
        pl.semaphore_signal(barrier, 1, device_id={"ctx": lax.rem(me + k, n_ctx)}, device_id_type=MESH)
    for copy in loads[:3]:
        copy.wait()

    lanes8 = lax.broadcasted_iota(jnp.int32, (8, 128), 1)
    rows8 = lax.broadcasted_iota(jnp.int32, (8, 128), 0)
    tile = jnp.zeros((8, 128), F32)
    for row, ref in enumerate((rate_ref, bias_ref, skip_ref)):
        for j in range(8):
            here = jnp.logical_and(rows8 == row, lanes8 == dp * 8 + j)
            tile = jnp.where(here, ref[j], tile)
    par_recv[dp] = tile

    pl.semaphore_wait(barrier, n_dp + n_ctx - 2)

    def to_all(src, dst, ss, rs, axis, size, index):
        for k in far_first(size):
            to(src(k), dst, ss.at[0], rs.at[0], {axis: lax.rem(index + k, size)}).start()

    to_all(lambda k: par_recv.at[dp], par_recv.at[dp], par_ss, par_rs, "dp", n_dp, dp)

    there = {"ctx": partner}
    pack_pair = to(pack_own, pack_other, pair_ss.at[0], pair_rs.at[0], there)
    x_pair = to(x_own, x_other, pair_ss.at[1], pair_rs.at[1], there)
    g_pair = to(g_own, g_other, pair_ss.at[2], pair_rs.at[2], there)
    half_groups = GROUPS // 2
    heads_here = HEADS // 2
    for copy in loads[3:]:
        copy.wait()
    pack_own[0:TOKENS, :] = b_ref[...].astype(F32)
    pack_own[TOKENS : 2 * TOKENS, :] = c_ref[...].astype(F32)
    pack_own[2 * TOKENS :, :] = raw_ref[pl.ds(pl.multiple_of((1 - core) * heads_here, heads_here), heads_here), :]
    pack_pair.start()

    def turned(src, dst, sent, half):
        for k in range(half_groups):
            rows = pl.ds(pl.multiple_of(half * HALF + k * GROUP_ROWS, GROUP_ROWS), GROUP_ROWS)
            value = jnp.transpose(src[:, rows].astype(F32))
            dst[rows, :] = value.astype(BF16)
            if sent is not None:
                sent[k * GROUP_ROWS : (k + 1) * GROUP_ROWS, :] = value

    turned(x_ref, xt, x_own, 1 - core)
    x_pair.start()
    turned(g_ref, gt, g_own, 1 - core)
    g_pair.start()
    turned(x_ref, xt, None, core)
    turned(g_ref, gt, None, core)
    gram_t[...] = mul_nt(b_ref[...], c_ref[...])

    seven = pl.ds(0, n_dp - 1)
    par_all = to(par_recv.at[seven], par_recv.at[seven], par_ss.at[0], par_rs.at[0], {"dp": dp})
    par_all.wait_recv()

    params = par_recv[0]
    for k in range(1, n_dp):
        params = params + par_recv[k]
    columns = jnp.transpose(jnp.concatenate([params] * 16, axis=0))[:HEADS, :]
    square = (HEADS, 128)
    rate = jnp.broadcast_to(columns[:, 0:1], square)
    bias = jnp.broadcast_to(columns[:, 1:2], square)
    skip_s[...] = jnp.broadcast_to(columns[:, 2:3], square)
    rate_s[...] = rate
    bias_s[...] = bias

    def steps_of(raw, rate, bias):
        z = raw + bias
        step = jnp.maximum(z, 0.0) + jnp.log1p(jnp.exp(-jnp.abs(z)))
        cum = lane_sums(-jnp.exp(rate) * step, False)
        return z, step, cum, jnp.broadcast_to(cum[:, 127:128], cum.shape)

    z, step, cum, last = steps_of(raw_ref[...], rate, bias)
    cum_s[...] = cum
    step_s[...] = step
    tail_s[...] = jnp.exp(last - cum) * step
    grow_s[...] = jnp.exp(cum)
    ends_own[...] = jnp.exp(last)
    here = pl.ds(pl.multiple_of(core * heads_here, heads_here), heads_here)
    pack_pair.wait()
    z_s[...] = z
    z_other, step_other, cum_o, last_o = steps_of(pack_other[2 * TOKENS :, :], rate_s[here, :], bias_s[here, :])
    z_o[...] = z_other
    step_o[...] = step_other
    tail_o[...] = jnp.exp(last_o - cum_o) * step_other
    grow_o[...] = jnp.exp(cum_o)
    ends_other[...] = jnp.exp(last_o)
    b_other = pack_other[0:TOKENS, :].astype(BF16)
    c_other = pack_other[TOKENS : 2 * TOKENS, :].astype(BF16)

    def rows_of(g):
        return pl.ds(pl.multiple_of(g * GROUP_ROWS, GROUP_ROWS), GROUP_ROWS)

    def heads_of(g):
        return pl.ds(pl.multiple_of(g * GROUP, GROUP), GROUP)

    outs = [
        pltpu.make_async_copy(src, dst, out_sem.at[k])
        for k, (src, dst) in enumerate(
            (
                (y_out, y_hbm), (dc_out, dc_hbm), (dt_out, dt_hbm), (dx_out, dx_hbm), (db_out, db_hbm),
                (total, total_got.at[chip]),
            )
        )
    ]

    mine = pl.ds(pl.multiple_of(core * HALF, HALF), HALF)
    base = core * (HEADS // 2)

    def row_of(ref, head):
        return jnp.broadcast_to(ref[pl.ds(head, 1), :], (WIDTH, 128))

    def two(ref, r):
        at = base + 2 * r if ref is ends_own else 2 * r
        return jnp.concatenate([row_of(ref, at), row_of(ref, at + 1)], axis=0)

    def piece_rows(r):
        return pl.ds(pl.multiple_of(core * HALF + r * PIECE, PIECE), PIECE)

    steps_away = [(dx, dy) for dx in range(4) for dy in range(4) if dx or dy]
    steps_away.sort(key=lambda step: -min(step[0], 4 - step[0]) - min(step[1], 4 - step[1]))
    far_chips = [lax.rem(chip // 4 + dx, 4) * 4 + lax.rem(chip + dy, 4) for dx, dy in steps_away]

    spot = pl.ds(pl.multiple_of(chip * PIECE, PIECE), PIECE)
    others = pl.ds(0, CHIPS - 1)
    most = pl.ds(0, HALF - PIECE)

    def out_pieces(src, dst, ss, rs):
        for target in far_chips:
            to(src.at[target], dst, ss.at[0], rs.at[0], {"ctx": target * 2 + core}).start()

    def all_pieces(src, ss, rs):
        return to(src.at[others], src.at[others], ss.at[0], rs.at[0], there)

    def product(rows, gains, entries):
        hi, lo = split(rows.astype(F32) * spread(gains))
        return mul(hi, entries) + mul(lo, entries)

    row = chip // 4

    def send(src, dst, ss, rs, g):
        for j in range(4):
            target = g * 4 + lax.rem(chip + j, 4)

            @pl.when(target != chip)
            def _():
                to(src.at[target], dst, ss.at[0], rs.at[0], {"ctx": target * 2 + core}).start()

    def totals_f(k, _):
        g = lax.rem(row + k + 1, 4)
        rows, heads = rows_of(core * half_groups + g), heads_of(core * half_groups + g)
        local_rows, local_heads = rows_of(g), heads_of(g)
        own = product(xt[rows, :], tail_s[heads, :], b_ref[...])
        other = product(x_other[local_rows, :], tail_o[local_heads, :], b_other)
        state[rows, :] = own
        state_other[local_rows, :] = other
        e_own, e_other = ends_own[heads, :], ends_other[local_heads, :]
        both = jnp.where(first, spread(e_other) * own + other, own + spread(e_own) * other)
        decay = e_own * e_other
        for j in range(4):
            tot_f[g * 4 + j, 0:PIECE, :] = both[j * PIECE : (j + 1) * PIECE, :]
            tot_f[g * 4 + j, PIECE : PIECE + 8, :] = jnp.concatenate([decay[2 * j : 2 * j + 2, :]] * 4, axis=0)
        send(tot_f, got_f.at[chip], f1_ss, f1_rs, g)
        return 0

    def totals_b(k, _):
        g = lax.rem(row + k + 1, 4)
        rows, heads = rows_of(core * half_groups + g), heads_of(core * half_groups + g)
        local_rows, local_heads = rows_of(g), heads_of(g)
        own = product(gt[rows, :], grow_s[heads, :], c_ref[...])
        other = product(g_other[local_rows, :], grow_o[local_heads, :], c_other)
        grad[rows, :] = own
        grad_other[local_rows, :] = other
        e_own, e_other = ends_own[heads, :], ends_other[local_heads, :]
        both = jnp.where(first, own + spread(e_own) * other, spread(e_other) * own + other)
        for j in range(4):
            tot_b[g * 4 + j] = both[j * PIECE : (j + 1) * PIECE, :]
        return 0

    x_pair.wait()
    lax.fori_loop(0, half_groups, totals_f, 0)
    got_f[chip] = tot_f[chip]
    g_pair.wait()
    lax.fori_loop(0, half_groups, totals_b, 0)
    got_b[chip] = tot_b[chip]

    def padded(value):
        return jnp.transpose(jnp.concatenate([value, value], axis=0))

    cum_t, step_t = padded(cum_s[...]), padded(step_s[...])
    for k in range(GROUPS):
        cum_col[k] = cum_t[:, k * GROUP : (k + 1) * GROUP]
        step_col[k] = step_t[:, k * GROUP : (k + 1) * GROUP]
    dgram_t[...] = jnp.zeros_like(dgram_t)

    def within(g, _):
        rows, heads = rows_of(g), heads_of(g)
        cum8, cumc, stepc = cum_s[heads, :], cum_col[g], step_col[g]
        xt8, gt8 = xt[rows, :], gt[rows, :]
        above = lax.broadcasted_iota(jnp.int32, (TOKENS, TOKENS), 0) <= lax.broadcasted_iota(
            jnp.int32, (TOKENS, TOKENS), 1
        )
        gram = gram_t[...]
        acc = dgram_t[...]
        none = jnp.zeros((WIDTH, TOKENS), BF16)
        for quad in range(2):
            xq = x_ref[:, pl.ds(pl.multiple_of(g * GROUP_ROWS + quad * 128, 128), 128)]
            for j in range(4):
                k = quad * 4 + j
                at = slice(k * WIDTH, (k + 1) * WIDTH)
                g_rows = gt8[at, :]
                weights_g = jnp.concatenate([g_rows if i == j else none for i in range(4)], axis=0)
                dw = mul(xq, weights_g)
                diff = jnp.broadcast_to(cum8[k : k + 1, :], (TOKENS, TOKENS)) - jnp.broadcast_to(
                    cumc[:, k : k + 1], (TOKENS, TOKENS)
                )
                seg = jnp.exp(jnp.where(above, diff, -1e30))
                factor = seg * jnp.broadcast_to(stepc[:, k : k + 1], (TOKENS, TOKENS))
                acc = acc + dw * factor
                hi, lo = split(gram * factor)
                inner = mul(xt8[at, :], hi) + mul(xt8[at, :], lo)
                back = mul_nt(g_rows, hi) + mul_nt(g_rows, lo)
                out = pl.ds(pl.multiple_of(g * GROUP_ROWS + k * WIDTH, WIDTH), WIDTH)
                y_t[out, :] = inner
                d_t[out, :] = back
        dgram_t[...] = acc
        x8, g8 = xt8.astype(F32), gt8.astype(F32)
        sk_s[heads, :] = folded(x8 * g8, GROUP)
        u_s[heads, :] = folded(g8 * y_t[rows, :], GROUP)
        vi_s[heads, :] = folded(x8 * d_t[rows, :], GROUP)
        return 0

    def turn_of(src, gains, hi_out, lo_out):
        def turn(g, _):
            rows, heads = rows_of(g), heads_of(g)
            hi, lo = split(jnp.transpose(src[rows, :].astype(F32) * spread(gains[heads, :])))
            hi_out[:, rows] = hi
            lo_out[:, rows] = lo
            return 0

        lax.fori_loop(0, GROUPS, turn, 0)

    lax.fori_loop(0, SPLIT[0], within, 0)
    f1_all = all_pieces(tot_f, f1_ss, f1_rs)
    f1_all.wait_send()
    out_pieces(tot_b, got_b.at[chip], b1_ss, b1_rs)

    lax.fori_loop(SPLIT[0], SPLIT[1], within, 0)

    def decay_of(q):
        return jnp.concatenate(
            [jnp.broadcast_to(got_f[q, PIECE + k : PIECE + k + 1, :], (WIDTH, 128)) for k in range(2)], axis=0
        )

    f1_all.wait_recv()
    run = jnp.zeros((PIECE, 128), F32)
    for q in range(CHIPS):
        pre_f[q] = run
        run = decay_of(q) * run + got_f[q, 0:PIECE, :]
    in_f[spot, :] = pre_f[chip]
    b1_all = all_pieces(tot_b, b1_ss, b1_rs)
    out_pieces(pre_f, in_f.at[spot], f2_ss, f2_rs)

    lax.fori_loop(SPLIT[1], SPLIT[2], within, 0)

    b1_all.wait_recv()
    run = jnp.zeros((PIECE, 128), F32)
    for q in reversed(range(CHIPS)):
        pre_b[q] = run
        run = decay_of(q) * run + got_b[q]
    in_b[spot, :] = pre_b[chip]
    all_pieces(pre_f, f2_ss, f2_rs).wait_send()
    for target in far_chips:
        to(pre_b.at[target], in_b.at[spot], b2_ss.at[0], b2_rs.at[row], {"ctx": target * 2 + core}).start()

    lax.fori_loop(SPLIT[2], GROUPS, within, 0)

    far = pl.ds(pl.multiple_of((1 - core) * heads_here, heads_here), heads_here)
    intra_own[0:heads_here, :] = u_s[far, :]
    intra_own[heads_here:, :] = vi_s[far, :]
    intra_pair = to(intra_own, intra_other, mid_ss.at[0], mid_rs.at[0], there)
    intra_pair.start()
    turn_of(gt, grow_s, egn_hi, egn_lo)
    turn_of(xt, tail_s, txn_hi, txn_lo)
    g_hi, g_lo = split(dgram_t[...])
    db_out[...] = mul(g_hi, c_ref[...]) + mul(g_lo, c_ref[...])
    t_hi, t_lo = split(jnp.transpose(dgram_t[...]))
    dc_out[...] = mul(t_hi, b_ref[...]) + mul(t_lo, b_ref[...])

    back_f_pair = to(back_f, carried.at[mine], back_ss.at[0], back_rs.at[0], there)
    back_b_pair = to(back_b, later.at[mine], back_ss.at[1], back_rs.at[1], there)
    to(in_f.at[most], in_f.at[most], f2_ss.at[0], f2_rs.at[0], there).wait_recv()
    for r in range(CHIPS):
        at = slice(r * PIECE, (r + 1) * PIECE)
        e_own, e_other = two(ends_own, r), two(ends_other, r)
        chips = in_f[at, :]
        carried[piece_rows(r), :] = jnp.where(first, chips, e_other * chips + state_other[at, :])
        back_f[at, :] = jnp.where(first, e_own * chips + state[piece_rows(r), :], chips)
    back_f_pair.start()
    def read(rows, heads):
        a_hi, a_lo = split(carried[rows, :])
        return spread(grow_s[heads, :]) * (mul_nt(a_hi, c_ref[...]) + mul_nt(a_lo, c_ref[...]))

    def own_f(k, _):
        g = core * half_groups + k
        rows, heads = rows_of(g), heads_of(g)
        part = read(rows, heads)
        y_t[rows, :] += part
        u_s[heads, :] += folded(gt[rows, :].astype(F32) * part, GROUP)
        return 0

    lax.fori_loop(0, half_groups, own_f, 0)
    intra_pair.wait()

    def other_f(g, _):
        rows, heads = rows_of(g), heads_of(g)
        a_hi, a_lo = split(back_f[rows, :])
        readout = mul_nt(a_hi, c_other) + mul_nt(a_lo, c_other)
        g8 = g_other[rows, :]
        u_o[heads, :] = intra_other[heads, :] + grow_o[heads, :] * folded(g8 * readout, GROUP)
        sk_o[heads, :] = folded(x_other[rows, :] * g8, GROUP)
        return 0

    lax.fori_loop(0, half_groups, other_f, 0)

    lanes8 = lax.broadcasted_iota(jnp.int32, (GROUP, 128), 1)

    def at_end(value):
        value = jnp.broadcast_to(jnp.sum(value, axis=1, keepdims=True), (GROUP, 128))
        return jnp.where(lanes8 == 127, value, 0.0)

    def from_later(l, gains, entries):
        l_hi, l_lo = split(l)
        return spread(gains) * (mul_nt(l_hi, entries) + mul_nt(l_lo, entries))

    def after_b(k, pieces):
        k = lax.rem(row + 3 - k, 4)
        part = in_b.at[pl.ds(0, pieces * PIECE)]
        to(part, part, b2_ss.at[0], b2_rs.at[k], there).wait_recv()
        g = core * half_groups + k
        rows, heads = rows_of(g), heads_of(g)
        near, few = rows_of(k), heads_of(k)
        chips = in_b[near, :]
        later[rows, :] = jnp.where(first, spread(ends_other[few, :]) * chips + grad_other[near, :], chips)
        back_b[near, :] = jnp.where(first, chips, spread(ends_own[heads, :]) * chips + grad[rows, :])
        l = later[rows, :]
        tq = from_later(l, tail_s[heads, :], b_ref[...])
        d_t[rows, :] += tq
        from_tail = folded(xt[rows, :].astype(F32) * tq, GROUP)
        v_s[heads, :] = vi_s[heads, :] + from_tail
        u_s[heads, :] += at_end(from_tail + ends_own[heads, :] * folded(carried[rows, :] * l, GROUP))
        rows, heads = near, few
        l = back_b[rows, :]
        from_tail = folded(x_other[rows, :] * from_later(l, tail_o[heads, :], b_other), GROUP)
        v_o[heads, :] = intra_other[pl.ds(pl.multiple_of(heads_here + k * GROUP, GROUP), GROUP), :] + from_tail
        u_o[heads, :] += at_end(from_tail + ends_other[heads, :] * folded(back_f[rows, :] * l, GROUP))

    def early_b(k, _):
        after_b(k, 4)
        return 0

    lax.fori_loop(0, half_groups - 1, early_b, 0)
    after_b(half_groups - 1, 3)
    back_b_pair.start()

    def pair_of(own, other):
        return jnp.concatenate([own[here, :], other[...]], axis=0)

    u, v, step, zs = pair_of(u_s, u_o), pair_of(v_s, v_o), pair_of(step_s, step_o), pair_of(z_s, z_o)
    rate_gain = jnp.exp(pair_of(rate_s, rate_s.at[here]))
    dlog = lane_sums(u - v, True)
    dstep = v / step - rate_gain * dlog
    draw = dstep / (1.0 + jnp.exp(-zs))
    rate_sum = jnp.sum(dlog * (-rate_gain * step), axis=1, keepdims=True)
    bias_sum = jnp.sum(draw, axis=1, keepdims=True)
    skip_sum = jnp.sum(pair_of(sk_s, sk_o), axis=1, keepdims=True)
    lanes = lax.broadcasted_iota(jnp.int32, square, 1)
    sums = jnp.where(lanes == 0, rate_sum, jnp.where(lanes == 1, bias_sum, jnp.where(lanes == 2, skip_sum, 0.0)))
    share[...] = sums[0:heads_here, :] + sums[heads_here:, :]

    owners = n_dp // 2
    owner = dp // owners == core
    for k in range(owners):
        plane = core * owners + k

        @pl.when(plane != dp)
        def _():
            to(share.at[k * 8 : k * 8 + 8], share_got.at[dp], share_ss.at[0], share_rs.at[0], {"dp": plane}).start()

        @pl.when(plane == dp)
        def _():
            share_got[dp] = share[k * 8 : k * 8 + 8, :]

    dt_out[here, :] = draw[0:heads_here, :]
    dt_sent[...] = draw[heads_here:, :]
    dt_pair = to(dt_sent, dt_out.at[here], mid_ss.at[1], mid_rs.at[1], there)
    dt_pair.start()

    def finish(g, _):
        rows, heads = rows_of(g), heads_of(g)
        gains = spread(skip_s[heads, :])
        y_out[:, rows] = jnp.transpose(y_t[rows, :] + gains * xt[rows, :].astype(F32)).astype(BF16)
        dx_out[:, rows] = jnp.transpose(d_t[rows, :] + gains * gt[rows, :].astype(F32)).astype(BF16)
        a_hi, a_lo = split(carried[rows, :])
        l_hi, l_lo = split(later[rows, :])
        dc_out[...] += mul(egn_hi[:, rows], a_hi) + mul(egn_hi[:, rows], a_lo) + mul(egn_lo[:, rows], a_hi)
        db_out[...] += mul(txn_hi[:, rows], l_hi) + mul(txn_hi[:, rows], l_lo) + mul(txn_lo[:, rows], l_hi)
        return 0

    def finish_far(k, _):
        g = (1 - core) * half_groups + k
        rows, heads = rows_of(g), heads_of(g)
        y_t[rows, :] += read(rows, heads)
        d_t[rows, :] += from_later(later[rows, :], tail_s[heads, :], b_ref[...])
        return finish(g, 0)

    def total_sums():
        @pl.when(owner)
        def _():
            to(share_got.at[seven], share_got.at[seven], share_ss.at[0], share_rs.at[0], {"dp": dp}).wait_recv()
            summed = share_got[0]
            for k in range(1, n_dp):
                summed = summed + share_got[k]
            total[...] = summed
            to_all(lambda k: total, total_got.at[chip], total_ss, total_rs, "ctx", n_ctx, me)
            outs[5].start()

    lax.fori_loop(core * half_groups, (core + 1) * half_groups, finish, 0)
    back_f_pair.wait()
    back_b_pair.wait()
    lax.fori_loop(0, FAR, finish_far, 0)
    total_sums()
    lax.fori_loop(FAR, half_groups, finish_far, 0)
    for k in (0, 1, 3, 4):
        outs[k].start()
    dt_pair.wait()
    outs[2].start()
    par_all.wait_send()
    b1_all.wait_send()
    all_pieces(pre_b, b2_ss, b2_rs).wait_send()
    for copy in outs[:5]:
        copy.wait()

    def tiles(ref, count):
        return ref.at[pl.ds(0, count)]

    def shares_sent(count):
        part = share.at[0 : count * 8]
        to(part, part, share_ss.at[0], share_rs.at[0], there).wait_send()

    def totals_got(count):
        part = tiles(total_got, count)
        to(part, part, total_ss.at[0], total_rs.at[0], there).wait_recv()

    @pl.when(owner)
    def _():
        shares_sent(owners - 1)
        outs[5].wait()
        part = state.at[0 : (n_ctx - 1) * 8]
        to(part, part, total_ss.at[0], total_rs.at[0], there).wait_send()
        totals_got(CHIPS - 1)

    @pl.when(jnp.logical_not(owner))
    def _():
        shares_sent(owners)
        totals_got(CHIPS)


def write(*refs):
    sources, targets, buffers, lines, in_sem, out_sem = refs[:6], refs[6:14], refs[14:20], refs[20], refs[21], refs[22]
    loads = [pltpu.make_async_copy(src, dst, in_sem.at[k]) for k, (src, dst) in enumerate(zip(sources, buffers))]
    loads = loads[5:] + loads[:5]
    for copy in loads:
        copy.start()
    kept = [*buffers[:5], lines.at[0], lines.at[1], lines.at[2]]
    stores = [pltpu.make_async_copy(src, dst, out_sem.at[k]) for k, (src, dst) in enumerate(zip(kept, targets))]
    loads[0].wait()
    totals = buffers[5]
    summed = totals[0]
    for k in range(1, totals.shape[0]):
        summed = summed + totals[k]
    turned = jnp.transpose(jnp.concatenate([summed] * 16, axis=0))
    for k in range(3):
        lines[k] = turned[k : k + 1, 0:8]
        stores[5 + k].start()
    for k in range(5):
        loads[1 + k].wait()
        stores[k].start()
    for copy in stores:
        copy.wait()


def local(x, b, c, raw, rate, bias, skip, g):
    n_dp = lax.axis_size("dp")
    vmem = pl.BlockSpec(memory_space=pltpu.VMEM)
    hbm = pl.BlockSpec(memory_space=pltpu.HBM)
    wide = (ROWS, 128)
    half = (HALF, 128)
    small = (HEADS, 128)
    piece = (CHIPS, PIECE, 128)
    longer = (CHIPS, PIECE + 8, 128)
    few = (HEADS // 2, 128)
    packed = (2 * TOKENS + HEADS // 2, 128)

    def buf(shape, dtype=F32):
        return pltpu.VMEM(shape, dtype)

    def sems(count):
        return pltpu.SemaphoreType.DMA((count,))

    landing = [
        buf((TOKENS, ROWS), BF16), buf((TOKENS, ROWS), BF16), buf((TOKENS, ENTRIES)), buf((TOKENS, ENTRIES)), buf(small),
        buf((CHIPS, 8, 128)),
    ]
    scratch = [
        *landing[:5],
        buf((TOKENS, ROWS), BF16), buf((TOKENS, ENTRIES), BF16), buf((TOKENS, ENTRIES), BF16), buf(small),
        buf((TOKENS, ROWS), BF16), *[pltpu.SMEM((8,), F32)] * 3,
        buf(wide, BF16), buf(wide, BF16), buf((TOKENS, TOKENS)), buf((n_dp, 8, 128)),
        *[buf(small)] * 5, buf((GROUPS, TOKENS, GROUP)), buf((GROUPS, TOKENS, GROUP)),
        *[buf((TOKENS, ROWS), BF16)] * 4, buf(small), buf(small),
        buf(packed), buf(half), buf(half), buf(packed), buf(half), buf(half), buf(few), buf(few),
        buf(small), buf(few), buf(wide), buf(wide), buf(half), buf(half),
        buf(longer), buf(piece), buf(longer), buf(piece),
        buf(piece), buf(piece), buf(half), buf(half), buf(half), buf(half), buf(wide), buf(wide),
        buf(wide), buf(wide), buf((TOKENS, TOKENS)), *[buf(small)] * 4, *[buf(few)] * 5, *[buf(small)] * 3, buf(few),
        buf(few), buf((n_dp, 8, 128)), buf((8, 128)),
        sems(8), sems(6), sems(1), sems(1), sems(2), sems(2), sems(3), sems(3), *[sems(1)] * 7, sems(4), sems(2), sems(2), *[sems(1)] * 4,
    ]
    wide_out = jax.ShapeDtypeStruct((TOKENS, ROWS), BF16)
    square_out = jax.ShapeDtypeStruct((TOKENS, ENTRIES), F32)
    dt_shape = jax.ShapeDtypeStruct((HEADS, TOKENS), F32)
    shapes = [wide_out, wide_out, square_out, square_out, dt_shape]
    results = pl.pallas_call(
        layer,
        out_shape=[*shapes, jax.ShapeDtypeStruct((CHIPS, 8, 128), F32)],
        in_specs=[hbm] * 8,
        out_specs=[hbm] * 6,
        scratch_shapes=scratch,
        compiler_params=pltpu.CompilerParams(collective_id=0, has_side_effects=True, vmem_limit_bytes=60 << 20),
        name="layer",
    )(x[0], b[0], c[0], raw[0], rate, bias, skip, g[0])
    y, dx, db, dc, dt, dr, dbias, dskip = pl.pallas_call(
        write,
        out_shape=[*shapes, *[jax.ShapeDtypeStruct((1, 8), F32)] * 3],
        in_specs=[hbm] * 6,
        out_specs=[hbm] * 8,
        scratch_shapes=[*landing, buf((3, 1, 8)), sems(6), sems(8)],
        compiler_params=pltpu.CompilerParams(vmem_limit_bytes=60 << 20),
        name="write",
    )(*results)
    return y[None], dx[None], db[None], dc[None], dt[None], dr.reshape(8), dbias.reshape(8), dskip.reshape(8)


def solution(mesh):
    tokens = P("dp", "ctx", None)
    strides = P("dp", None, "ctx")
    owned = P("dp")
    return jax.shard_map(
        local,
        mesh=mesh,
        in_specs=(tokens, tokens, tokens, strides, owned, owned, owned, tokens),
        out_specs=(tokens, tokens, tokens, tokens, strides, owned, owned, owned),
        check_vma=False,
    )
```

```python
import jax
import jax.numpy as jnp
from jax import lax
from jax.experimental import pallas as pl
from jax.experimental.pallas import tpu as pltpu
from jax.sharding import PartitionSpec as P

MESH = pl.DeviceIdType.MESH
F32, BF16 = jnp.float32, jnp.bfloat16

TOKENS = 128
HEADS = 64
WIDTH = 32
ENTRIES = 128
ROWS = HEADS * WIDTH
HALF = ROWS // 2
GROUP = 8
GROUP_ROWS = GROUP * WIDTH
GROUPS = HEADS // GROUP
CHIPS = 16
PIECE = HALF // CHIPS


def split(value):
    high = value.astype(BF16)
    return high, (value - high.astype(F32)).astype(BF16)


def mul(a, b):
    return jnp.dot(a, b, preferred_element_type=F32)


def mul_nt(a, b):
    return lax.dot_general(a, b, (((1,), (1,)), ((), ())), preferred_element_type=F32)


def spread(rows, width=WIDTH):
    count = rows.shape[0]
    parts = [jnp.broadcast_to(rows[k : k + 1, :], (width, rows.shape[1])) for k in range(count)]
    return jnp.concatenate(parts, axis=0)


def folded(value, count):
    return jnp.sum(value.reshape(count, WIDTH, value.shape[1]), axis=1)


def lane_sums(value, reverse):
    lanes = lax.broadcasted_iota(jnp.int32, value.shape, 1)
    size = value.shape[1]
    shift = 1
    while shift < size:
        if reverse:
            moved = jnp.where(lanes < size - shift, pltpu.roll(value, size - shift, 1), 0.0)
        else:
            moved = jnp.where(lanes >= shift, pltpu.roll(value, shift, 1), 0.0)
        value = value + moved
        shift *= 2
    return value
SPLIT = (0, 3, 5)
FAR = 1


def far_first(size):
    return sorted(range(1, size), key=lambda k: -min(k, size - k))


def layer(
    x_hbm, b_hbm, c_hbm, raw_hbm, rate_hbm, bias_hbm, skip_hbm, g_hbm,
    y_hbm, dx_hbm, db_hbm, dc_hbm, dt_hbm, total_got,
    y_out, dx_out, db_out, dc_out, dt_out,
    x_ref, b_ref, c_ref, raw_ref, g_ref, rate_ref, bias_ref, skip_ref,
    xt, gt, gram_t, par_recv, cum_s, step_s, tail_s, grow_s, skip_s, cum_col, step_col,
    txn_hi, txn_lo, egn_hi, egn_lo, rate_s, bias_s, pack_own, x_own, g_own, pack_other, x_other, g_other, tail_o, grow_o,
    ends_own, ends_other, state, grad, state_other, grad_other,
    tot_f, tot_b, got_f, got_b, pre_f, pre_b, in_f, in_b, back_f, back_b, carried, later,
    y_t, d_t, dgram_t, u_s, v_s, sk_s, z_s, z_o, step_o, u_o, v_o, sk_o, vi_s, intra_own, intra_other, dt_sent, share, share_got, total,
    in_sem, out_sem, par_ss, par_rs, mid_ss, mid_rs, pair_ss, pair_rs, f1_ss, f1_rs, b1_ss, b1_rs, f2_ss, f2_rs, b2_ss, b2_rs,
    back_ss, back_rs, share_ss, share_rs, total_ss, total_rs,
):
    me = lax.axis_index("ctx")
    dp = lax.axis_index("dp")
    n_dp = lax.axis_size("dp")
    n_ctx = lax.axis_size("ctx")
    core = lax.rem(me, 2)
    chip = me // 2
    partner = chip * 2 + 1 - core
    first = core == 0

    def to(src, dst, ss, rs, where):
        return pltpu.make_async_remote_copy(src, dst, ss, rs, device_id=where, device_id_type=MESH)

    loads = [
        pltpu.make_async_copy(src, dst, in_sem.at[k])
        for k, (src, dst) in enumerate(
            (
                (rate_hbm, rate_ref), (bias_hbm, bias_ref), (skip_hbm, skip_ref), (raw_hbm, raw_ref),
                (x_hbm, x_ref), (b_hbm, b_ref), (g_hbm, g_ref), (c_hbm, c_ref),
            )
        )
    ]
    for copy in loads:
        copy.start()
    barrier = pltpu.get_barrier_semaphore()
    for k in far_first(n_dp):
        pl.semaphore_signal(barrier, 1, device_id={"dp": lax.rem(dp + k, n_dp)}, device_id_type=MESH)
    for k in far_first(n_ctx):
        pl.semaphore_signal(barrier, 1, device_id={"ctx": lax.rem(me + k, n_ctx)}, device_id_type=MESH)
    for copy in loads[:3]:
        copy.wait()

    lanes8 = lax.broadcasted_iota(jnp.int32, (8, 128), 1)
    rows8 = lax.broadcasted_iota(jnp.int32, (8, 128), 0)
    tile = jnp.zeros((8, 128), F32)
    for row, ref in enumerate((rate_ref, bias_ref, skip_ref)):
        for j in range(8):
            here = jnp.logical_and(rows8 == row, lanes8 == dp * 8 + j)
            tile = jnp.where(here, ref[j], tile)
    par_recv[dp] = tile

    pl.semaphore_wait(barrier, n_dp + n_ctx - 2)

    def to_all(src, dst, ss, rs, axis, size, index):
        for k in far_first(size):
            to(src(k), dst, ss.at[0], rs.at[0], {axis: lax.rem(index + k, size)}).start()

    to_all(lambda k: par_recv.at[dp], par_recv.at[dp], par_ss, par_rs, "dp", n_dp, dp)

    there = {"ctx": partner}
    pack_pair = to(pack_own, pack_other, pair_ss.at[0], pair_rs.at[0], there)
    x_pair = to(x_own, x_other, pair_ss.at[1], pair_rs.at[1], there)
    g_pair = to(g_own, g_other, pair_ss.at[2], pair_rs.at[2], there)
    half_groups = GROUPS // 2
    heads_here = HEADS // 2
    for copy in loads[3:]:
        copy.wait()
    pack_own[0:TOKENS, :] = b_ref[...].astype(F32)
    pack_own[TOKENS : 2 * TOKENS, :] = c_ref[...].astype(F32)
    pack_own[2 * TOKENS :, :] = raw_ref[pl.ds(pl.multiple_of((1 - core) * heads_here, heads_here), heads_here), :]
    pack_pair.start()

    def turned(src, dst, sent, half):
        for k in range(half_groups):
            rows = pl.ds(pl.multiple_of(half * HALF + k * GROUP_ROWS, GROUP_ROWS), GROUP_ROWS)
            value = jnp.transpose(src[:, rows].astype(F32))
            dst[rows, :] = value.astype(BF16)
            if sent is not None:
                sent[k * GROUP_ROWS : (k + 1) * GROUP_ROWS, :] = value

    turned(x_ref, xt, x_own, 1 - core)
    x_pair.start()
    turned(g_ref, gt, g_own, 1 - core)
    g_pair.start()
    turned(x_ref, xt, None, core)
    turned(g_ref, gt, None, core)
    gram_t[...] = mul_nt(b_ref[...], c_ref[...])

    seven = pl.ds(0, n_dp - 1)
    par_all = to(par_recv.at[seven], par_recv.at[seven], par_ss.at[0], par_rs.at[0], {"dp": dp})
    par_all.wait_recv()

    params = par_recv[0]
    for k in range(1, n_dp):
        params = params + par_recv[k]
    columns = jnp.transpose(jnp.concatenate([params] * 16, axis=0))[:HEADS, :]
    square = (HEADS, 128)
    rate = jnp.broadcast_to(columns[:, 0:1], square)
    bias = jnp.broadcast_to(columns[:, 1:2], square)
    skip_s[...] = jnp.broadcast_to(columns[:, 2:3], square)
    rate_s[...] = rate
    bias_s[...] = bias

    def steps_of(raw, rate, bias):
        z = raw + bias
        step = jnp.maximum(z, 0.0) + jnp.log1p(jnp.exp(-jnp.abs(z)))
        cum = lane_sums(-jnp.exp(rate) * step, False)
        return z, step, cum, jnp.broadcast_to(cum[:, 127:128], cum.shape)

    z, step, cum, last = steps_of(raw_ref[...], rate, bias)
    cum_s[...] = cum
    step_s[...] = step
    tail_s[...] = jnp.exp(last - cum) * step
    grow_s[...] = jnp.exp(cum)
    ends_own[...] = jnp.exp(last)
    here = pl.ds(pl.multiple_of(core * heads_here, heads_here), heads_here)
    pack_pair.wait()
    z_s[...] = z
    z_other, step_other, cum_o, last_o = steps_of(pack_other[2 * TOKENS :, :], rate_s[here, :], bias_s[here, :])
    z_o[...] = z_other
    step_o[...] = step_other
    tail_o[...] = jnp.exp(last_o - cum_o) * step_other
    grow_o[...] = jnp.exp(cum_o)
    ends_other[...] = jnp.exp(last_o)
    b_other = pack_other[0:TOKENS, :].astype(BF16)
    c_other = pack_other[TOKENS : 2 * TOKENS, :].astype(BF16)

    def rows_of(g):
        return pl.ds(pl.multiple_of(g * GROUP_ROWS, GROUP_ROWS), GROUP_ROWS)

    def heads_of(g):
        return pl.ds(pl.multiple_of(g * GROUP, GROUP), GROUP)

    outs = [
        pltpu.make_async_copy(src, dst, out_sem.at[k])
        for k, (src, dst) in enumerate(
            (
                (y_out, y_hbm), (dc_out, dc_hbm), (dt_out, dt_hbm), (dx_out, dx_hbm), (db_out, db_hbm),
                (total, total_got.at[chip]),
            )
        )
    ]

    mine = pl.ds(pl.multiple_of(core * HALF, HALF), HALF)
    base = core * (HEADS // 2)

    def row_of(ref, head):
        return jnp.broadcast_to(ref[pl.ds(head, 1), :], (WIDTH, 128))

    def two(ref, r):
        at = base + 2 * r if ref is ends_own else 2 * r
        return jnp.concatenate([row_of(ref, at), row_of(ref, at + 1)], axis=0)

    def piece_rows(r):
        return pl.ds(pl.multiple_of(core * HALF + r * PIECE, PIECE), PIECE)

    steps_away = [(dx, dy) for dx in range(4) for dy in range(4) if dx or dy]
    steps_away.sort(key=lambda step: -min(step[0], 4 - step[0]) - min(step[1], 4 - step[1]))
    far_chips = [lax.rem(chip // 4 + dx, 4) * 4 + lax.rem(chip + dy, 4) for dx, dy in steps_away]

    spot = pl.ds(pl.multiple_of(chip * PIECE, PIECE), PIECE)
    others = pl.ds(0, CHIPS - 1)
    most = pl.ds(0, HALF - PIECE)

    def out_pieces(src, dst, ss, rs):
        for target in far_chips:
            to(src.at[target], dst, ss.at[0], rs.at[0], {"ctx": target * 2 + core}).start()

    def all_pieces(src, ss, rs):
        return to(src.at[others], src.at[others], ss.at[0], rs.at[0], there)

    def product(rows, gains, entries):
        hi, lo = split(rows.astype(F32) * spread(gains))
        return mul(hi, entries) + mul(lo, entries)

    row = chip // 4

    def send(src, dst, ss, rs, g):
        for j in range(4):
            target = g * 4 + lax.rem(chip + j, 4)

            @pl.when(target != chip)
            def _():
                to(src.at[target], dst, ss.at[0], rs.at[0], {"ctx": target * 2 + core}).start()

    def totals_f(k, _):
        g = lax.rem(row + k + 1, 4)
        rows, heads = rows_of(core * half_groups + g), heads_of(core * half_groups + g)
        local_rows, local_heads = rows_of(g), heads_of(g)
        own = product(xt[rows, :], tail_s[heads, :], b_ref[...])
        other = product(x_other[local_rows, :], tail_o[local_heads, :], b_other)
        state[rows, :] = own
        state_other[local_rows, :] = other
        e_own, e_other = ends_own[heads, :], ends_other[local_heads, :]
        both = jnp.where(first, spread(e_other) * own + other, own + spread(e_own) * other)
        decay = e_own * e_other
        for j in range(4):
            tot_f[g * 4 + j, 0:PIECE, :] = both[j * PIECE : (j + 1) * PIECE, :]
            tot_f[g * 4 + j, PIECE : PIECE + 8, :] = jnp.concatenate([decay[2 * j : 2 * j + 2, :]] * 4, axis=0)
        send(tot_f, got_f.at[chip], f1_ss, f1_rs, g)
        return 0

    def totals_b(k, _):
        g = lax.rem(row + k + 1, 4)
        rows, heads = rows_of(core * half_groups + g), heads_of(core * half_groups + g)
        local_rows, local_heads = rows_of(g), heads_of(g)
        own = product(gt[rows, :], grow_s[heads, :], c_ref[...])
        other = product(g_other[local_rows, :], grow_o[local_heads, :], c_other)
        grad[rows, :] = own
        grad_other[local_rows, :] = other
        e_own, e_other = ends_own[heads, :], ends_other[local_heads, :]
        both = jnp.where(first, own + spread(e_own) * other, spread(e_other) * own + other)
        for j in range(4):
            tot_b[g * 4 + j] = both[j * PIECE : (j + 1) * PIECE, :]
        return 0

    x_pair.wait()
    lax.fori_loop(0, half_groups, totals_f, 0)
    got_f[chip] = tot_f[chip]
    g_pair.wait()
    lax.fori_loop(0, half_groups, totals_b, 0)
    got_b[chip] = tot_b[chip]

    def padded(value):
        return jnp.transpose(jnp.concatenate([value, value], axis=0))

    cum_t, step_t = padded(cum_s[...]), padded(step_s[...])
    for k in range(GROUPS):
        cum_col[k] = cum_t[:, k * GROUP : (k + 1) * GROUP]
        step_col[k] = step_t[:, k * GROUP : (k + 1) * GROUP]
    dgram_t[...] = jnp.zeros_like(dgram_t)

    def within(g, _):
        rows, heads = rows_of(g), heads_of(g)
        cum8, cumc, stepc = cum_s[heads, :], cum_col[g], step_col[g]
        xt8, gt8 = xt[rows, :], gt[rows, :]
        above = lax.broadcasted_iota(jnp.int32, (TOKENS, TOKENS), 0) <= lax.broadcasted_iota(
            jnp.int32, (TOKENS, TOKENS), 1
        )
        gram = gram_t[...]
        acc = dgram_t[...]
        none = jnp.zeros((WIDTH, TOKENS), BF16)
        for quad in range(2):
            xq = x_ref[:, pl.ds(pl.multiple_of(g * GROUP_ROWS + quad * 128, 128), 128)]
            for j in range(4):
                k = quad * 4 + j
                at = slice(k * WIDTH, (k + 1) * WIDTH)
                g_rows = gt8[at, :]
                weights_g = jnp.concatenate([g_rows if i == j else none for i in range(4)], axis=0)
                dw = mul(xq, weights_g)
                diff = jnp.broadcast_to(cum8[k : k + 1, :], (TOKENS, TOKENS)) - jnp.broadcast_to(
                    cumc[:, k : k + 1], (TOKENS, TOKENS)
                )
                seg = jnp.exp(jnp.where(above, diff, -1e30))
                factor = seg * jnp.broadcast_to(stepc[:, k : k + 1], (TOKENS, TOKENS))
                acc = acc + dw * factor
                hi, lo = split(gram * factor)
                inner = mul(xt8[at, :], hi) + mul(xt8[at, :], lo)
                back = mul_nt(g_rows, hi) + mul_nt(g_rows, lo)
                out = pl.ds(pl.multiple_of(g * GROUP_ROWS + k * WIDTH, WIDTH), WIDTH)
                y_t[out, :] = inner
                d_t[out, :] = back
        dgram_t[...] = acc
        x8, g8 = xt8.astype(F32), gt8.astype(F32)
        sk_s[heads, :] = folded(x8 * g8, GROUP)
        u_s[heads, :] = folded(g8 * y_t[rows, :], GROUP)
        vi_s[heads, :] = folded(x8 * d_t[rows, :], GROUP)
        return 0

    def turn_of(src, gains, hi_out, lo_out):
        def turn(g, _):
            rows, heads = rows_of(g), heads_of(g)
            hi, lo = split(jnp.transpose(src[rows, :].astype(F32) * spread(gains[heads, :])))
            hi_out[:, rows] = hi
            lo_out[:, rows] = lo
            return 0

        lax.fori_loop(0, GROUPS, turn, 0)

    lax.fori_loop(0, SPLIT[0], within, 0)
    f1_all = all_pieces(tot_f, f1_ss, f1_rs)
    f1_all.wait_send()
    out_pieces(tot_b, got_b.at[chip], b1_ss, b1_rs)

    lax.fori_loop(SPLIT[0], SPLIT[1], within, 0)

    def decay_of(q):
        return jnp.concatenate(
            [jnp.broadcast_to(got_f[q, PIECE + k : PIECE + k + 1, :], (WIDTH, 128)) for k in range(2)], axis=0
        )

    f1_all.wait_recv()
    run = jnp.zeros((PIECE, 128), F32)
    for q in range(CHIPS):
        pre_f[q] = run
        run = decay_of(q) * run + got_f[q, 0:PIECE, :]
    in_f[spot, :] = pre_f[chip]
    b1_all = all_pieces(tot_b, b1_ss, b1_rs)
    out_pieces(pre_f, in_f.at[spot], f2_ss, f2_rs)

    lax.fori_loop(SPLIT[1], SPLIT[2], within, 0)

    b1_all.wait_recv()
    run = jnp.zeros((PIECE, 128), F32)
    for q in reversed(range(CHIPS)):
        pre_b[q] = run
        run = decay_of(q) * run + got_b[q]
    in_b[spot, :] = pre_b[chip]
    all_pieces(pre_f, f2_ss, f2_rs).wait_send()
    for target in far_chips:
        to(pre_b.at[target], in_b.at[spot], b2_ss.at[0], b2_rs.at[row], {"ctx": target * 2 + core}).start()

    lax.fori_loop(SPLIT[2], GROUPS, within, 0)

    far = pl.ds(pl.multiple_of((1 - core) * heads_here, heads_here), heads_here)
    intra_own[0:heads_here, :] = u_s[far, :]
    intra_own[heads_here:, :] = vi_s[far, :]
    intra_pair = to(intra_own, intra_other, mid_ss.at[0], mid_rs.at[0], there)
    intra_pair.start()
    turn_of(gt, grow_s, egn_hi, egn_lo)
    turn_of(xt, tail_s, txn_hi, txn_lo)
    g_hi, g_lo = split(dgram_t[...])
    db_out[...] = mul(g_hi, c_ref[...]) + mul(g_lo, c_ref[...])
    t_hi, t_lo = split(jnp.transpose(dgram_t[...]))
    dc_out[...] = mul(t_hi, b_ref[...]) + mul(t_lo, b_ref[...])

    back_f_pair = to(back_f, carried.at[mine], back_ss.at[0], back_rs.at[0], there)
    back_b_pair = to(back_b, later.at[mine], back_ss.at[1], back_rs.at[1], there)
    to(in_f.at[most], in_f.at[most], f2_ss.at[0], f2_rs.at[0], there).wait_recv()
    for r in range(CHIPS):
        at = slice(r * PIECE, (r + 1) * PIECE)
        e_own, e_other = two(ends_own, r), two(ends_other, r)
        chips = in_f[at, :]
        carried[piece_rows(r), :] = jnp.where(first, chips, e_other * chips + state_other[at, :])
        back_f[at, :] = jnp.where(first, e_own * chips + state[piece_rows(r), :], chips)
    back_f_pair.start()
    def read(rows, heads):
        a_hi, a_lo = split(carried[rows, :])
        return spread(grow_s[heads, :]) * (mul_nt(a_hi, c_ref[...]) + mul_nt(a_lo, c_ref[...]))

    def own_f(k, _):
        g = core * half_groups + k
        rows, heads = rows_of(g), heads_of(g)
        part = read(rows, heads)
        y_t[rows, :] += part
        u_s[heads, :] += folded(gt[rows, :].astype(F32) * part, GROUP)
        return 0

    lax.fori_loop(0, half_groups, own_f, 0)
    intra_pair.wait()

    def other_f(g, _):
        rows, heads = rows_of(g), heads_of(g)
        a_hi, a_lo = split(back_f[rows, :])
        readout = mul_nt(a_hi, c_other) + mul_nt(a_lo, c_other)
        g8 = g_other[rows, :]
        u_o[heads, :] = intra_other[heads, :] + grow_o[heads, :] * folded(g8 * readout, GROUP)
        sk_o[heads, :] = folded(x_other[rows, :] * g8, GROUP)
        return 0

    lax.fori_loop(0, half_groups, other_f, 0)

    lanes8 = lax.broadcasted_iota(jnp.int32, (GROUP, 128), 1)

    def pair_of(own, other):
        return jnp.concatenate([own[here, :], other[...]], axis=0)

    rate_gain = jnp.exp(pair_of(rate_s, rate_s.at[here]))
    slope = 1.0 / (1.0 + jnp.exp(-pair_of(z_s, z_o)))
    weight = slope / pair_of(step_s, step_o)
    reach = rate_gain * lane_sums(slope, False)
    cum_both = jnp.concatenate([cum_s[here, :], cum_o], axis=0)

    def at_end(value):
        value = jnp.broadcast_to(jnp.sum(value, axis=1, keepdims=True), (GROUP, 128))
        return jnp.where(lanes8 == 127, value, 0.0)

    def from_later(l, gains, entries):
        l_hi, l_lo = split(l)
        return spread(gains) * (mul_nt(l_hi, entries) + mul_nt(l_lo, entries))

    def after_b(k, pieces):
        k = lax.rem(row + 3 - k, 4)
        part = in_b.at[pl.ds(0, pieces * PIECE)]
        to(part, part, b2_ss.at[0], b2_rs.at[k], there).wait_recv()
        g = core * half_groups + k
        rows, heads = rows_of(g), heads_of(g)
        near, few = rows_of(k), heads_of(k)
        chips = in_b[near, :]
        later[rows, :] = jnp.where(first, spread(ends_other[few, :]) * chips + grad_other[near, :], chips)
        back_b[near, :] = jnp.where(first, chips, spread(ends_own[heads, :]) * chips + grad[rows, :])
        l = later[rows, :]
        tq = from_later(l, tail_s[heads, :], b_ref[...])
        d_t[rows, :] += tq
        from_tail = folded(xt[rows, :].astype(F32) * tq, GROUP)
        v_s[heads, :] = vi_s[heads, :] + from_tail
        u_s[heads, :] += at_end(from_tail + ends_own[heads, :] * folded(carried[rows, :] * l, GROUP))
        rows, heads = near, few
        l = back_b[rows, :]
        from_tail = folded(x_other[rows, :] * from_later(l, tail_o[heads, :], b_other), GROUP)
        v_o[heads, :] = intra_other[pl.ds(pl.multiple_of(heads_here + k * GROUP, GROUP), GROUP), :] + from_tail
        u_o[heads, :] += at_end(from_tail + ends_other[heads, :] * folded(back_f[rows, :] * l, GROUP))

    def early_b(k, _):
        after_b(k, 4)
        return 0

    lax.fori_loop(0, half_groups - 1, early_b, 0)
    after_b(half_groups - 1, 3)
    back_b_pair.start()

    u, v = pair_of(u_s, u_o), pair_of(v_s, v_o)
    dcum = u - v
    rate_sum = jnp.sum(dcum * cum_both, axis=1, keepdims=True)
    bias_sum = jnp.sum(v * weight - dcum * reach, axis=1, keepdims=True)
    skip_sum = jnp.sum(pair_of(sk_s, sk_o), axis=1, keepdims=True)
    lanes = lax.broadcasted_iota(jnp.int32, square, 1)
    sums = jnp.where(lanes == 0, rate_sum, jnp.where(lanes == 1, bias_sum, jnp.where(lanes == 2, skip_sum, 0.0)))
    share[...] = sums[0:heads_here, :] + sums[heads_here:, :]

    owners = n_dp // 2
    owner = dp // owners == core
    for k in range(owners):
        plane = core * owners + k

        @pl.when(plane != dp)
        def _():
            to(share.at[k * 8 : k * 8 + 8], share_got.at[dp], share_ss.at[0], share_rs.at[0], {"dp": plane}).start()

        @pl.when(plane == dp)
        def _():
            share_got[dp] = share[k * 8 : k * 8 + 8, :]

    draw = weight * v - slope * rate_gain * lane_sums(dcum, True)
    dt_out[here, :] = draw[0:heads_here, :]
    dt_sent[...] = draw[heads_here:, :]
    dt_pair = to(dt_sent, dt_out.at[here], mid_ss.at[1], mid_rs.at[1], there)
    dt_pair.start()

    def finish(g, _):
        rows, heads = rows_of(g), heads_of(g)
        gains = spread(skip_s[heads, :])
        y_out[:, rows] = jnp.transpose(y_t[rows, :] + gains * xt[rows, :].astype(F32)).astype(BF16)
        dx_out[:, rows] = jnp.transpose(d_t[rows, :] + gains * gt[rows, :].astype(F32)).astype(BF16)
        a_hi, a_lo = split(carried[rows, :])
        l_hi, l_lo = split(later[rows, :])
        dc_out[...] += mul(egn_hi[:, rows], a_hi) + mul(egn_hi[:, rows], a_lo) + mul(egn_lo[:, rows], a_hi)
        db_out[...] += mul(txn_hi[:, rows], l_hi) + mul(txn_hi[:, rows], l_lo) + mul(txn_lo[:, rows], l_hi)
        return 0

    def finish_far(k, _):
        g = (1 - core) * half_groups + k
        rows, heads = rows_of(g), heads_of(g)
        y_t[rows, :] += read(rows, heads)
        d_t[rows, :] += from_later(later[rows, :], tail_s[heads, :], b_ref[...])
        return finish(g, 0)

    def total_sums():
        @pl.when(owner)
        def _():
            to(share_got.at[seven], share_got.at[seven], share_ss.at[0], share_rs.at[0], {"dp": dp}).wait_recv()
            summed = share_got[0]
            for k in range(1, n_dp):
                summed = summed + share_got[k]
            total[...] = summed
            to_all(lambda k: total, total_got.at[chip], total_ss, total_rs, "ctx", n_ctx, me)
            outs[5].start()

    lax.fori_loop(core * half_groups, (core + 1) * half_groups, finish, 0)
    back_f_pair.wait()
    back_b_pair.wait()
    lax.fori_loop(0, FAR, finish_far, 0)
    total_sums()
    lax.fori_loop(FAR, half_groups, finish_far, 0)
    for k in (0, 1, 3, 4):
        outs[k].start()
    dt_pair.wait()
    outs[2].start()
    par_all.wait_send()
    b1_all.wait_send()
    all_pieces(pre_b, b2_ss, b2_rs).wait_send()
    for copy in outs[:5]:
        copy.wait()

    def tiles(ref, count):
        return ref.at[pl.ds(0, count)]

    def shares_sent(count):
        part = share.at[0 : count * 8]
        to(part, part, share_ss.at[0], share_rs.at[0], there).wait_send()

    def totals_got(count):
        part = tiles(total_got, count)
        to(part, part, total_ss.at[0], total_rs.at[0], there).wait_recv()

    @pl.when(owner)
    def _():
        shares_sent(owners - 1)
        outs[5].wait()
        part = state.at[0 : (n_ctx - 1) * 8]
        to(part, part, total_ss.at[0], total_rs.at[0], there).wait_send()
        totals_got(CHIPS - 1)

    @pl.when(jnp.logical_not(owner))
    def _():
        shares_sent(owners)
        totals_got(CHIPS)


def write(*refs):
    sources, targets, buffers, lines, in_sem, out_sem = refs[:6], refs[6:14], refs[14:20], refs[20], refs[21], refs[22]
    loads = [pltpu.make_async_copy(src, dst, in_sem.at[k]) for k, (src, dst) in enumerate(zip(sources, buffers))]
    loads = loads[5:] + loads[:5]
    for copy in loads:
        copy.start()
    kept = [*buffers[:5], lines.at[0], lines.at[1], lines.at[2]]
    stores = [pltpu.make_async_copy(src, dst, out_sem.at[k]) for k, (src, dst) in enumerate(zip(kept, targets))]
    loads[0].wait()
    totals = buffers[5]
    summed = totals[0]
    for k in range(1, totals.shape[0]):
        summed = summed + totals[k]
    turned = jnp.transpose(jnp.concatenate([summed] * 16, axis=0))
    for k in range(3):
        lines[k] = turned[k : k + 1, 0:8]
        stores[5 + k].start()
    for k in range(5):
        loads[1 + k].wait()
        stores[k].start()
    for copy in stores:
        copy.wait()


def local(x, b, c, raw, rate, bias, skip, g):
    n_dp = lax.axis_size("dp")
    vmem = pl.BlockSpec(memory_space=pltpu.VMEM)
    hbm = pl.BlockSpec(memory_space=pltpu.HBM)
    wide = (ROWS, 128)
    half = (HALF, 128)
    small = (HEADS, 128)
    piece = (CHIPS, PIECE, 128)
    longer = (CHIPS, PIECE + 8, 128)
    few = (HEADS // 2, 128)
    packed = (2 * TOKENS + HEADS // 2, 128)

    def buf(shape, dtype=F32):
        return pltpu.VMEM(shape, dtype)

    def sems(count):
        return pltpu.SemaphoreType.DMA((count,))

    landing = [
        buf((TOKENS, ROWS), BF16), buf((TOKENS, ROWS), BF16), buf((TOKENS, ENTRIES)), buf((TOKENS, ENTRIES)), buf(small),
        buf((CHIPS, 8, 128)),
    ]
    scratch = [
        *landing[:5],
        buf((TOKENS, ROWS), BF16), buf((TOKENS, ENTRIES), BF16), buf((TOKENS, ENTRIES), BF16), buf(small),
        buf((TOKENS, ROWS), BF16), *[pltpu.SMEM((8,), F32)] * 3,
        buf(wide, BF16), buf(wide, BF16), buf((TOKENS, TOKENS)), buf((n_dp, 8, 128)),
        *[buf(small)] * 5, buf((GROUPS, TOKENS, GROUP)), buf((GROUPS, TOKENS, GROUP)),
        *[buf((TOKENS, ROWS), BF16)] * 4, buf(small), buf(small),
        buf(packed), buf(half), buf(half), buf(packed), buf(half), buf(half), buf(few), buf(few),
        buf(small), buf(few), buf(wide), buf(wide), buf(half), buf(half),
        buf(longer), buf(piece), buf(longer), buf(piece),
        buf(piece), buf(piece), buf(half), buf(half), buf(half), buf(half), buf(wide), buf(wide),
        buf(wide), buf(wide), buf((TOKENS, TOKENS)), *[buf(small)] * 4, *[buf(few)] * 5, *[buf(small)] * 3, buf(few),
        buf(few), buf((n_dp, 8, 128)), buf((8, 128)),
        sems(8), sems(6), sems(1), sems(1), sems(2), sems(2), sems(3), sems(3), *[sems(1)] * 7, sems(4), sems(2), sems(2), *[sems(1)] * 4,
    ]
    wide_out = jax.ShapeDtypeStruct((TOKENS, ROWS), BF16)
    square_out = jax.ShapeDtypeStruct((TOKENS, ENTRIES), F32)
    dt_shape = jax.ShapeDtypeStruct((HEADS, TOKENS), F32)
    shapes = [wide_out, wide_out, square_out, square_out, dt_shape]
    results = pl.pallas_call(
        layer,
        out_shape=[*shapes, jax.ShapeDtypeStruct((CHIPS, 8, 128), F32)],
        in_specs=[hbm] * 8,
        out_specs=[hbm] * 6,
        scratch_shapes=scratch,
        compiler_params=pltpu.CompilerParams(collective_id=0, has_side_effects=True, vmem_limit_bytes=60 << 20),
        name="layer",
    )(x[0], b[0], c[0], raw[0], rate, bias, skip, g[0])
    y, dx, db, dc, dt, dr, dbias, dskip = pl.pallas_call(
        write,
        out_shape=[*shapes, *[jax.ShapeDtypeStruct((1, 8), F32)] * 3],
        in_specs=[hbm] * 6,
        out_specs=[hbm] * 8,
        scratch_shapes=[*landing, buf((3, 1, 8)), sems(6), sems(8)],
        compiler_params=pltpu.CompilerParams(vmem_limit_bytes=60 << 20),
        name="write",
    )(*results)
    return y[None], dx[None], db[None], dc[None], dt[None], dr.reshape(8), dbias.reshape(8), dskip.reshape(8)


def solution(mesh):
    tokens = P("dp", "ctx", None)
    strides = P("dp", None, "ctx")
    owned = P("dp")
    return jax.shard_map(
        local,
        mesh=mesh,
        in_specs=(tokens, tokens, tokens, strides, owned, owned, owned, tokens),
        out_specs=(tokens, tokens, tokens, tokens, strides, owned, owned, owned),
        check_vma=False,
    )
```
